32 devices in a mesh: gx: 8 (over z, x), gy: 4 (over y, core).
Axes of the slice: x: 2, y: 2, z: 4, core: 2. Of those that a mesh axis runs over, the one named last changes fastest.
Arguments:
- probes: bfloat16 [48, 4, 128, 1024], P(None, None, 'gx', 'gy'), may hold values from -6 to 6
- classes: int32 [4, 128, 1024], P(None, 'gx', 'gy'), may hold values from 0 to 7
- class_table: float32 [8], replicated, may hold values from 0.3 to 3
- weights: float32 [4, 128, 1024], P(None, 'gx', 'gy'), may hold values from 5 to 500
- prior_block: float32 [1024, 256], P('gy'), may hold values from -0.1875 to 0.1875
- prior_left: float32 [8, 16, 1024], P(None, None, 'gy'), may hold values from -1.5 to 1.5
- prior_right: float32 [8, 16, 1024], P(None, None, 'gy'), may hold values from -6 to 6
- block_ranks: int32 [8], replicated, may hold values from 4 to 16
Outputs:
- basis: float32 [48, 4, 128, 1024], P(None, None, 'gx', 'gy')
- projected: float32 [48, 48], replicated
The draws below stay inside these ranges and needn't reach their ends.
All inputs are finite; a program needn't handle non-finite values.
Results may differ from the reference program's by a relative error of at most 0.0018.
Values may be sent and summed in bfloat16 or wider, within the bound.
No kernel may reach another device: no remote copies, remote signals or barrier semaphores. Data moves between devices by JAX's collectives and lax.ppermute only.
A program may use at most 64 MiB of HBM per device.

```python
import math
import jax
import jax.numpy as jnp
from jax import lax

K = 48
NZ = 4
CY = 256
NCLASS = 8
R = 16
LEVMAX = 8
NX = 128
NY = 1024
CELLS = 524288
N_GY = 4


def place_ends(values, rng, smallest, top_value):
    extent = values.shape
    spot = [jax.random.randint(jax.random.fold_in(rng, axis), (), 0, extent[axis]) for axis in range(len(extent))]
    values = values.at[tuple(spot)].set(smallest)
    longest = extent.index(max(extent))
    spot[longest] = (spot[longest] + 1) % extent[longest]
    return values.at[tuple(spot)].set(top_value)


def block_scale(own_key, shape, pieces, least, largest):
    factor_of = 1.0
    for position, shards_of in pieces:
        draws = jax.random.uniform(jax.random.fold_in(jax.random.fold_in(own_key, 6), position), (shards_of,), jnp.float32, least / len(pieces), largest / len(pieces))
        factor_of = factor_of * jnp.repeat(jnp.exp(draws), shape[position] // shards_of).reshape((-1,) + (1,) * (len(shape) - 1 - position))
    return factor_of


def centred(rng, shape, spread, reach, pieces=(), kind=jnp.bfloat16):
    gain = block_scale(rng, shape, pieces, -0.22, 0.18) if pieces else 1.0
    values = jax.random.normal(rng, shape, jnp.float32) * spread * gain
    return jnp.minimum(jnp.maximum(values, -reach), reach).astype(kind)


def setup_inputs(seed: int = 0) -> dict:
    streams_of = jax.random.split(jax.random.key(seed), 9)
    return {
        "probes": centred(streams_of[0], (K, NZ, NX, NY), 1.0, 6.0, ((2, 8), (3, 4))),
        "classes": place_ends(jax.random.randint(streams_of[1], (NZ, NX, NY), 0, NCLASS), jax.random.fold_in(streams_of[1], 1), 0, NCLASS - 1).astype(jnp.int32),
        "class_table": jnp.clip(jnp.exp(jax.random.uniform(streams_of[2], (NCLASS,), jnp.float32, math.log(0.3), math.log(3.0))), 0.3, 3.0),
        "weights": jnp.clip(jnp.exp(math.log(500.0) - 4.6051702 * jax.random.uniform(streams_of[3], (NZ, NX, NY), jnp.float32) ** block_scale(streams_of[3], (NZ, NX, NY), ((1, 8), (2, 4)), -0.2, 0.2)), 5.0, 500.0),
        "prior_block": centred(streams_of[4], (NY, CY), (4 * CY) ** -0.5, 0.1875, ((0, 4),), jnp.float32),
        "prior_left": centred(streams_of[5], (LEVMAX, R, NY), R ** -0.5, 1.5, ((2, 4),), jnp.float32),
        "prior_right": centred(streams_of[6], (LEVMAX, R, NY), 1.0, 6.0, ((2, 4),), jnp.float32),
        "block_ranks": place_ends(jax.random.randint(streams_of[7], (LEVMAX,), R // 4, R + 1), jax.random.fold_in(streams_of[7], 1), R // 4, R).astype(jnp.int32),
    }


HIGH = lax.Precision.HIGHEST

def face_parts(cond_ext):
    centre = cond_ext[:, 1:-1, 1:-1]
    padded_z = jnp.pad(centre, ((1, 1), (0, 0), (0, 0)))
    face_terms = [0.5 * (centre + cond_ext[:, 2:, 1:-1]), 0.5 * (centre + cond_ext[:, :-2, 1:-1]), 0.5 * (centre + cond_ext[:, 1:-1, 2:]), 0.5 * (centre + cond_ext[:, 1:-1, :-2]), 0.5 * (centre + padded_z[2:]), 0.5 * (centre + padded_z[:-2])]
    diagonal_part = 1.0 + face_terms[0] + face_terms[1] + face_terms[2] + face_terms[3] + face_terms[4] + face_terms[5]
    return (face_terms, diagonal_part)

def neighbour_sum(values_ext, face_terms):
    padded_z = jnp.pad(values_ext[:, :, 1:-1, 1:-1], ((0, 0), (1, 1), (0, 0), (0, 0)))
    others = [values_ext[:, :, 2:, 1:-1], values_ext[:, :, :-2, 1:-1], values_ext[:, :, 1:-1, 2:], values_ext[:, :, 1:-1, :-2], padded_z[:, 2:], padded_z[:, :-2]]
    total = face_terms[0] * others[0]
    for index in range(1, 6):
        total = total + face_terms[index] * others[index]
    return total

def pad_plane(values):
    return jnp.pad(values, ((0, 0), (0, 0), (1, 1), (1, 1)))

def prior_apply(field, prior_block, prior_left, prior_right, block_ranks):
    line_rows = field.reshape(NZ * NX, NY)
    row_count = NZ * NX
    leaf_count = NY // CY
    blocks = line_rows.reshape(row_count, leaf_count, CY)
    full_block = prior_block.reshape(leaf_count, CY, CY) + jnp.eye(CY, dtype=jnp.float32)[None]
    result = jnp.einsum('pbj,bij->pbi', blocks, full_block, precision=HIGH).reshape(row_count, NY)
    level_count = N_GY.bit_length() - 1
    rank_index = jnp.arange(R, dtype=jnp.int32)
    for level_index in range(level_count):
        group = CY * 2 ** (level_index + 1)
        half = group // 2
        groups = NY // group
        split_rows = line_rows.reshape(row_count, groups, 2, half)
        right_part = prior_right[level_index].reshape(R, groups, 2, half)
        left_part = prior_left[level_index].reshape(R, groups, 2, half)
        rank_mask = (rank_index < block_ranks[level_index]).astype(jnp.float32) * float(CY * 2 ** level_index) ** (-0.5)
        coefficients = jnp.einsum('pgah,rgah->pgar', split_rows, right_part, precision=HIGH) * rank_mask
        swapped = coefficients[:, :, ::-1, :]
        result = result + jnp.einsum('pgar,rgah->pgah', swapped, left_part, precision=HIGH).reshape(row_count, NY)
    return result.reshape(NZ, NX, NY)

def reference(probes, classes, class_table, weights, prior_block, prior_left, prior_right, block_ranks):
    conductivity = class_table[classes]
    cond_pad = jnp.pad(conductivity, ((0, 0), (1, 1), (1, 1)))
    face_terms, diagonal_part = face_parts(cond_pad)

    def sketch_one(probe):
        source = probe.astype(jnp.float32)[None]
        first_fwd = source / diagonal_part
        second_fwd = (source + neighbour_sum(pad_plane(first_fwd), face_terms)) / diagonal_part
        misfit = weights * second_fwd
        first_adj = misfit / diagonal_part
        second_adj = (misfit + neighbour_sum(pad_plane(first_adj), face_terms)) / diagonal_part
        return (second_adj + source)[0]
    sketch = lax.map(sketch_one, probes)
    flattened = sketch.reshape(K, -1)
    gram_matrix = jnp.dot(flattened, flattened.T, precision=HIGH) / float(CELLS)
    lower_factor = jnp.linalg.cholesky(gram_matrix)
    inverse = jax.scipy.linalg.solve_triangular(lower_factor, jnp.eye(K, dtype=jnp.float32), lower=True)
    basis_flat = jnp.dot(inverse, flattened, precision=HIGH)
    basis = basis_flat.reshape(K, NZ, NX, NY)

    def project_one(field):
        applied = prior_apply(field, prior_block, prior_left, prior_right, block_ranks)
        return jnp.dot(basis_flat, applied.reshape(-1), precision=HIGH)
    rows = lax.map(project_one, basis)
    projected = rows.T / float(CELLS)
    return (basis, projected)
```

```python
import functools
import jax
import jax.numpy as jnp
from jax import lax
from jax.experimental import pallas as pl
from jax.experimental.pallas import tpu as pltpu
from jax.sharding import PartitionSpec as P

HIGH = lax.Precision.HIGHEST
F32 = jnp.float32
BF16 = jnp.bfloat16
LANES = 128
SUB = 8
GROUP = 32
REACH = 3
AUX = 16
VMEM = pl.BlockSpec(memory_space=pltpu.VMEM)
ANY = pl.BlockSpec(memory_space=pl.ANY)


def lanes_of(shape):
    return lax.broadcasted_iota(jnp.int32, shape, len(shape) - 1)


def halves(v):
    hi = v.astype(BF16)
    return hi, (v - hi.astype(F32)).astype(BF16)


def nt(a, b, precision=None):
    return lax.dot_general(a, b, (((1,), (1,)), ((), ())), precision=precision, preferred_element_type=F32)


def pack_kernel(K, NZ, X, p_ref, cls_ref, w_ref, pt_ref, ylo_ref, yhi_ref, xlo_ref, xhi_ref, edge, aux):
    rows, ext = NZ * X, X + 4
    for k in range(K):
        v = p_ref[k * rows : (k + 1) * rows, :].astype(F32)
        for z in range(NZ):
            for h in range(2):
                pt_ref[h, pl.ds((z * ext + 2) * K + k, X, stride=K), :] = v[z * X : (z + 1) * X, h * LANES : (h + 1) * LANES]
    lane = lanes_of((SUB, LANES))
    for kt in range(K // SUB):
        out = [jnp.zeros((SUB, LANES), F32) for _ in range(4)]
        for z in range(NZ):
            for x in range(X):
                row = (z * ext + 2 + x) * K + kt * SUB
                to = z * GROUP + x + REACH
                here = lane == to
                left, right = pt_ref[0, row : row + SUB, :], pt_ref[1, row : row + SUB, :]
                for i, (tile, col) in enumerate(((left, 0), (left, 1), (right, LANES - 1), (right, LANES - 2))):
                    out[i] = jnp.where(here, pltpu.roll(tile, (to - col) % LANES, 1), out[i])
        edge[0, kt * SUB : (kt + 1) * SUB, :] = out[0]
        edge[1, kt * SUB : (kt + 1) * SUB, :] = out[1]
        edge[2, kt * SUB : (kt + 1) * SUB, :] = out[2]
        edge[3, kt * SUB : (kt + 1) * SUB, :] = out[3]
    for side, ref in enumerate((ylo_ref, yhi_ref)):
        for d in range(2):
            ref[d * K : (d + 1) * K, :] = edge[2 * side + d, :K, :].astype(BF16)
    wide = lanes_of((LANES, LANES))
    turned = []
    for source in (cls_ref, w_ref):
        edge[0] = jnp.zeros((LANES, LANES), F32)
        for z in range(NZ):
            v = source[z * X : (z + 1) * X, :].astype(F32)
            if source is cls_ref:
                v = v + 1.0
            edge[0, z * GROUP + REACH : z * GROUP + REACH + X, :] = jnp.where(lanes_of((X, LANES)) < 64, v[:, :LANES], v[:, LANES:])
        turned.append(edge[0].T)
    for side, ref in enumerate((ylo_ref, yhi_ref)):
        at = (0, 1, 2) if side == 0 else (LANES - 1, LANES - 2, LANES - 3)
        aux[...] = jnp.zeros_like(aux)
        for d in range(3):
            aux[d : d + 1, :LANES] = turned[0][at[d] : at[d] + 1, :]
        w_hi, w_lo = halves(turned[1][at[0] : at[0] + 1, :])
        aux[3:4, :LANES] = w_hi.astype(F32)
        aux[4:5, :LANES] = w_lo.astype(F32)
        ref[2 * K : 2 * K + AUX, :] = aux[:AUX, :LANES].astype(BF16)
    for side, ref in enumerate((xlo_ref, xhi_ref)):
        first = 0 if side == 0 else X - 2
        for z in range(NZ):
            for i in range(2):
                row = (z * ext + 2 + first + i) * K
                for h in range(2):
                    ref[(z * 2 + i) * K : (z * 2 + i + 1) * K, h * LANES : (h + 1) * LANES] = pt_ref[h, row : row + K, :].astype(BF16)
        aux[...] = jnp.zeros_like(aux)
        for z in range(NZ):
            c0 = z * X + (0 if side == 0 else X - 3)
            aux[z * SUB : z * SUB + 3, :] = cls_ref[c0 : c0 + 3, :].astype(F32) + 1.0
            w0 = z * X + (0 if side == 0 else X - 1)
            w_hi, w_lo = halves(w_ref[w0 : w0 + 1, :])
            aux[z * SUB + 3 : z * SUB + 4, :] = w_hi.astype(F32)
            aux[z * SUB + 4 : z * SUB + 5, :] = w_lo.astype(F32)
        ref[2 * NZ * K : 2 * NZ * K + NZ * SUB, :] = aux[...].astype(BF16)


def merged(own, from_left, from_right):
    X = GROUP // 2
    m = lanes_of(own.shape) % GROUP
    left = pltpu.roll(from_left, LANES - X, 1)
    right = pltpu.roll(from_right, X, 1)
    out = jnp.where(m < X + REACH, own, jnp.where(m < X + 2 * REACH, right, 0.0))
    return jnp.where(m < REACH, left, out)


def main_kernel(
    K, NZ, X, levels, R,
    table_ref, pt_in, xl_ref, xr_ref, yl_ref, yr_ref, rl_ref, rr_ref, ylo_ref, yhi_ref, cls_ref, w_ref, block_ref, factor_ref,
    s_ref, v_ref, u_ref, gx_ref, pt_ref, t_ref, cg, wg, rg, cf, hp, ht,
):
    ext, wide = X + 4, X + 2
    KT = K // SUB
    sq = (LANES, LANES)
    lane_sq = lanes_of(sq)
    for z in range(NZ):
        for i in range(2):
            for h in range(2):
                cut = (slice((z * 2 + i) * K, (z * 2 + i + 1) * K), slice(h * LANES, (h + 1) * LANES))
                pt_ref[h, (z * ext + i) * K : (z * ext + i + 1) * K, :] = xl_ref[cut].astype(F32)
                at = z * ext + X + 2 + i
                pt_ref[h, at * K : (at + 1) * K, :] = xr_ref[cut].astype(F32)
    y_aux = [ref[2 * K : 2 * K + AUX, :].astype(F32) for ref in (yl_ref, yr_ref)]
    x_aux = [ref[2 * NZ * K : 2 * NZ * K + NZ * SUB, :].astype(F32) for ref in (xl_ref, xr_ref)]
    sides = []
    for side in range(2):
        own = y_aux[side]
        a = rl_ref[side, 2 * K : 2 * K + AUX, :].astype(F32)
        b = rr_ref[side, 2 * K : 2 * K + AUX, :].astype(F32)
        sides.append(merged(own, a, b))
    spread = jnp.zeros(sq, F32)
    row_sq = lax.broadcasted_iota(jnp.int32, sq, 0)
    spread_w = jnp.zeros(sq, F32)
    for side in range(2):
        at = (LANES - 1, LANES - 2, LANES - 3) if side == 0 else (0, 1, 2)
        for d in range(3):
            spread = jnp.where(row_sq == at[d], sides[side][d : d + 1, :], spread)
        spread_w = jnp.where(row_sq == at[0], sides[side][3:4, :] + sides[side][4:5, :], spread_w)
    y_class, y_weight = spread.T, spread_w.T
    keep = (lane_sq >= LANES // 2, lane_sq < LANES // 2)
    cg[0] = jnp.where(keep[0], y_class, 0.0)
    cg[3] = jnp.where(keep[1], y_class, 0.0)
    wg[0] = jnp.where(keep[0], y_weight, 0.0)
    wg[3] = jnp.where(keep[1], y_weight, 0.0)
    for h in range(2):
        lo = slice(h * LANES, (h + 1) * LANES)
        cg[1 + h] = jnp.zeros(sq, F32)
        wg[1 + h] = jnp.zeros(sq, F32)
        for z in range(NZ):
            g = z * GROUP
            cg[1 + h, g + REACH : g + REACH + X, :] = cls_ref[z * X : (z + 1) * X, lo].astype(F32) + 1.0
            cg[1 + h, g : g + REACH, :] = x_aux[0][z * SUB : z * SUB + 3, lo]
            cg[1 + h, g + REACH + X : g + 2 * REACH + X, :] = x_aux[1][z * SUB : z * SUB + 3, lo]
            wg[1 + h, g + REACH : g + REACH + X, :] = w_ref[z * X : (z + 1) * X, lo]
            wg[1 + h, g + REACH - 1 : g + REACH, :] = x_aux[0][z * SUB + 3 : z * SUB + 4, lo] + x_aux[0][z * SUB + 4 : z * SUB + 5, lo]
            wg[1 + h, g + REACH + X : g + REACH + X + 1, :] = x_aux[1][z * SUB + 3 : z * SUB + 4, lo] + x_aux[1][z * SUB + 4 : z * SUB + 5, lo]
    for t in range(4):
        ids = cg[t]
        cond = jnp.zeros(sq, F32)
        for j in range(table_ref.shape[0]):
            cond = jnp.where(ids == float(j + 1), table_ref[j], cond)
        cg[t] = cond

    zeros_g = jnp.zeros((GROUP, LANES), F32)

    def ahead(ref, t):
        nxt = ref[t + 1] if t < 3 else jnp.zeros(sq, F32)
        return jnp.where(lane_sq == LANES - 1, pltpu.roll(nxt, LANES - 1, 1), pltpu.roll(ref[t], LANES - 1, 1))

    def behind(ref, t):
        prv = ref[t - 1] if t > 0 else jnp.zeros(sq, F32)
        return jnp.where(lane_sq == 0, pltpu.roll(prv, 1, 1), pltpu.roll(ref[t], 1, 1))

    def around(ref, t):
        v = ref[t]
        return [
            pltpu.roll(v, LANES - 1, 0),
            pltpu.roll(v, 1, 0),
            ahead(ref, t),
            behind(ref, t),
            jnp.concatenate([v[GROUP:], zeros_g], 0),
            jnp.concatenate([zeros_g, v[:-GROUP]], 0),
        ]

    for t in range(4):
        c = cg[t]
        total = jnp.ones(sq, F32)
        for other in around(cg, t):
            total = total + 0.5 * (c + other)
        rg[t] = 1.0 / total
    picked = jnp.zeros(sq, F32)
    for t in range(4):
        c, r, w = cg[t], rg[t], wg[t]
        pairs = zip(around(cg, t), around(rg, t))
        terms = [r] + [0.5 * (c + c_n) * (r * r_n) for c_n, r_n in pairs]
        for j, term in enumerate(terms):
            if t in (1, 2):
                cf[j, t - 1] = w * term
                cf[7 + j, t - 1] = term
            else:
                to = j if t == 0 else 8 + j
                start = LANES - 1 if t == 0 else 0
                picked = jnp.where(lane_sq == to, pltpu.roll(w * term, (to - start) % LANES, 1), picked)
    edge_cf = picked.T
    for side, (recv, mine) in enumerate(((yl_ref, ylo_ref), (yr_ref, yhi_ref))):
        p1 = merged(recv[:K, :].astype(F32), rl_ref[side, :K, :].astype(F32), rr_ref[side, :K, :].astype(F32))
        p2 = recv[K : 2 * K, :].astype(F32)
        p0 = mine[:K, :].astype(F32)
        y_next, y_prev = (p0, p2) if side == 0 else (p2, p0)
        parts = [
            p1,
            pltpu.roll(p1, LANES - 1, 1),
            pltpu.roll(p1, 1, 1),
            y_next,
            y_prev,
            pltpu.roll(p1, LANES - GROUP, 1),
            pltpu.roll(p1, GROUP, 1),
        ]
        total = edge_cf[8 * side : 8 * side + 1, :] * parts[0]
        for j in range(1, 7):
            total = total + edge_cf[8 * side + j : 8 * side + j + 1, :] * parts[j]
        hp[side] = p1
        ht[side] = total

    lane = lanes_of((SUB, LANES))
    is_first, is_last = lane == 0, lane == LANES - 1

    def stencil(z, coef_row, first_cf, src, centre_row, x_step, z_step, halo, kt):
        row = pl.multiple_of(centre_row + kt * SUB, SUB)
        c = [src[h, pl.ds(row, SUB), :] for h in range(2)]
        up = [src[h, pl.ds(row + x_step, SUB), :] for h in range(2)]
        down = [src[h, pl.ds(row - x_step, SUB), :] for h in range(2)]
        hl = pltpu.roll(halo[0, kt * SUB : (kt + 1) * SUB, :], LANES - coef_row, 1)
        hr = pltpu.roll(halo[1, kt * SUB : (kt + 1) * SUB, :], LANES - 1 - coef_row, 1)
        fwd = [pltpu.roll(v, LANES - 1, 1) for v in c]
        bwd = [pltpu.roll(v, 1, 1) for v in c]
        nxt = [jnp.where(is_last, fwd[1], fwd[0]), jnp.where(is_last, hr, fwd[1])]
        prv = [jnp.where(is_first, hl, bwd[0]), jnp.where(is_first, bwd[0], bwd[1])]
        out = []
        for h in range(2):
            co = [cf[first_cf + j, h, pl.ds(coef_row, 1), :] for j in range(7)]
            acc = co[0] * c[h] + co[1] * up[h] + co[2] * down[h] + co[3] * nxt[h] + co[4] * prv[h]
            if z < NZ - 1:
                acc = acc + co[5] * src[h, pl.ds(row + z_step, SUB), :]
            if z > 0:
                acc = acc + co[6] * src[h, pl.ds(row - z_step, SUB), :]
            out.append(acc)
        return row, out

    def stage_one(i, carry):
        for z in range(NZ):
            for kt in range(KT):
                _, out = stencil(z, z * GROUP + i + 2, 0, pt_ref, (z * ext + i + 1) * K, K, ext * K, hp, kt)
                to = pl.multiple_of((z * wide + i) * K + kt * SUB, SUB)
                for h in range(2):
                    t_ref[h, pl.ds(to, SUB), :] = out[h]
        return carry

    lax.fori_loop(0, wide, stage_one, 0)

    lane_k = lanes_of((K, LANES))

    def stage_two(i, carry):
        gram, mixed = carry
        places = [[jnp.zeros((K, LANES), F32) for _ in range(levels)] for _ in range(2)]
        for half in range(2):
            x = 2 * i + half
            his = []
            for z in range(NZ):
                lines = []
                for kt in range(KT):
                    _, out = stencil(z, z * GROUP + x + REACH, 7, t_ref, (z * wide + x + 1) * K, K, wide * K, ht, kt)
                    row = pl.multiple_of((z * ext + x + 2) * K + kt * SUB, SUB)
                    to = pl.multiple_of((z * X + x) * K + kt * SUB, SUB)
                    both = []
                    for h in range(2):
                        s = out[h] + pt_ref[h, pl.ds(row, SUB), :]
                        s_ref[h, pl.ds(to, SUB), :] = s
                        both.append(s)
                    lines.append(jnp.concatenate(both, 1))
                line = jnp.concatenate(lines, 0)
                hi, lo = halves(line)
                gram = gram + nt(hi, jnp.concatenate([hi, lo], 0))
                his.append(hi)
            stack = jnp.concatenate(his, 0)
            leaf = nt(stack, block_ref[...]).astype(BF16)
            coef = nt(stack, factor_ref[...])
            for z in range(NZ):
                mixed = mixed + nt(his[z], leaf[z * K : (z + 1) * K])
                part = coef[z * K : (z + 1) * K]
                at = half * NZ * R + z * R
                here = (lane_k >= at) & (lane_k < at + R)
                for q in range(2):
                    for l in range(levels):
                        moved = pltpu.roll(part, (at - (q * levels + l) * R) % LANES, 1)
                        places[q][l] = jnp.where(here, moved, places[q][l])
        for l in range(levels):
            v_ref[l, i] = places[0][l].astype(BF16)
            u_ref[l, i] = places[1][l].astype(BF16)
        return gram, mixed

    gram, mixed = lax.fori_loop(0, X // 2, stage_two, (jnp.zeros((K, 2 * K), F32), jnp.zeros((K, K), F32)))
    low = gram[:, K:]
    gx_ref[...] = jnp.zeros_like(gx_ref)
    gx_ref[:, :K] = gram[:, :K] + low + low.T
    gx_ref[:, LANES // 2 : LANES // 2 + K] = mixed


def couple_kernel(K, level_of, gx_ref, u_ref, *refs):
    sib_refs, out_ref = refs[:-1], refs[-1]
    total = jnp.zeros((K, K), F32)
    sums = {}
    for l, ref in zip(level_of, sib_refs):
        sums.setdefault(l, []).append(ref)
    for l, group in sums.items():
        for i in range(u_ref.shape[1]):
            v = group[0][i].astype(F32)
            for ref in group[1:]:
                v = v + ref[i].astype(F32)
            total = total + nt(u_ref[l, i], v.astype(BF16))
    out_ref[...] = gx_ref[...]
    at = LANES // 2
    out_ref[:, at : at + K] = gx_ref[:, at : at + K] + total


def finish_kernel(K, NZ, X, cells, gx_ref, s_ref, basis_ref, proj_ref, out, sem):
    lane = lanes_of((K, LANES))
    row = lax.broadcasted_iota(jnp.int32, (K, LANES), 0)
    half = LANES // 2
    gx = gx_ref[...] * (1.0 / cells)
    gram = gx[:, :K]
    mixed = gram + gx[:, half : half + K]
    aug = jnp.where(lane < K, gx, jnp.where(lane - half == row, 1.0, 0.0))
    for j in range(K - 1):
        pivot_row = aug[j : j + 1, :]
        factor = aug[:, j : j + 1] * (1.0 / aug[j : j + 1, j : j + 1])
        aug = aug - jnp.where(row > j, factor, 0.0) * pivot_row
    pivots = jnp.sum(jnp.where(lane == row, aug, 0.0), axis=1, keepdims=True)
    inverse = aug[:, half : half + K] * lax.rsqrt(pivots)
    left = jnp.dot(inverse, mixed, precision=HIGH, preferred_element_type=F32)
    proj_ref[...] = nt(left, inverse, precision=HIGH)
    i_hi, i_lo = halves(inverse)
    lhs = jnp.concatenate([i_hi, i_lo, i_hi], 1)
    W = 2 * LANES
    copies = []
    for z in range(NZ):

        def line(x, carry, z=z):
            at = pl.multiple_of((z * X + x) * K, SUB)
            s = jnp.concatenate([s_ref[h, pl.ds(at, K), :] for h in range(2)], 1)
            hi, lo = halves(s)
            b = jnp.dot(lhs, jnp.concatenate([hi, hi, lo], 0), preferred_element_type=F32)
            for h in range(2):
                out[h, z, pl.ds(x, K, stride=X), :] = b[:, h * LANES : (h + 1) * LANES]
            return carry

        lax.fori_loop(0, X, line, 0)
        for h in range(2):
            for part in range(1):
                copies.append(
                    pltpu.make_async_copy(
                        out.at[h, z].reshape(K, X, LANES), basis_ref.at[:, z, :, pl.ds(h * LANES, LANES)], sem.at[z, h]
                    )
                )
                copies[-1].start()
    for c in copies:
        c.wait()


def exchanged(v, axis, bits):
    return lax.ppermute(v, axis, [(i, i ^ bits) for i in range(lax.axis_size(axis))])


def shifted(v, axis, by):
    n = lax.axis_size(axis)
    return lax.ppermute(v, axis, [(i, i + by) for i in range(n) if 0 <= i + by < n])


def summed(v):
    for axis in ("gx", "gy"):
        bit = 1
        while bit < lax.axis_size(axis):
            v = v + exchanged(v, axis, bit)
            bit *= 2
    return v


def shards(probes, classes, class_table, weights, prior_block, prior_left, prior_right, block_ranks):
    K, NZ, X, W = probes.shape
    R = prior_left.shape[1]
    levels = lax.axis_size("gy").bit_length() - 1
    cells = float(NZ * X * W * lax.axis_size("gx") * lax.axis_size("gy"))
    rows, ext, wide = NZ * X, X + 4, X + 2
    shape = jax.ShapeDtypeStruct
    cls2, w2 = classes.reshape(rows, W), weights.reshape(rows, W)
    params = functools.partial(pltpu.CompilerParams, vmem_limit_bytes=32 << 20)
    y_rows, x_rows = 2 * K + AUX, 2 * NZ * K + NZ * SUB
    pt, ylo, yhi, xlo, xhi = pl.pallas_call(
        functools.partial(pack_kernel, K, NZ, X),
        out_shape=(
            shape((2, NZ * ext * K, LANES), F32),
            shape((y_rows, LANES), BF16),
            shape((y_rows, LANES), BF16),
            shape((x_rows, W), BF16),
            shape((x_rows, W), BF16),
        ),
        in_specs=[VMEM] * 3,
        out_specs=(VMEM,) * 5,
        scratch_shapes=[pltpu.VMEM((4, LANES, LANES), F32), pltpu.VMEM((NZ * SUB, W), F32)],
        compiler_params=params(),
        name="pack",
    )(probes.reshape(K * rows, W), cls2, w2)
    xl, xr = shifted(xhi, "gx", 1), shifted(xlo, "gx", -1)
    yl, yr = shifted(yhi, "gy", 1), shifted(ylo, "gy", -1)
    both = jnp.stack([yl, yr])
    rl, rr = shifted(both, "gx", 1), shifted(both, "gx", -1)
    scale = jnp.array([float(W * 2**l) ** -0.5 for l in range(levels)], F32)
    mask = (jnp.arange(R, dtype=jnp.int32)[None, :] < block_ranks[:levels, None]).astype(F32) * scale[:, None]
    right = prior_right[:levels] * mask[:, :, None]
    factor = jnp.concatenate([right, prior_left[:levels]], 0).reshape(2 * levels * R, W)
    if 2 * levels * R < LANES:
        factor = jnp.pad(factor, ((0, LANES - 2 * levels * R), (0, 0)))
    slab = (2, rows * K, LANES)
    side = (levels, X // 2, K, LANES)
    s, v, u, gx, _ = pl.pallas_call(
        functools.partial(main_kernel, K, NZ, X, levels, R),
        out_shape=(
            shape(slab, F32),
            shape(side, BF16),
            shape(side, BF16),
            shape((K, LANES), F32),
            shape(pt.shape, F32),
        ),
        in_specs=[pl.BlockSpec(memory_space=pltpu.SMEM)] + [VMEM] * 13,
        out_specs=(VMEM,) * 5,
        scratch_shapes=[
            pltpu.VMEM((2, NZ * wide * K, LANES), F32),
            pltpu.VMEM((4, LANES, LANES), F32),
            pltpu.VMEM((4, LANES, LANES), F32),
            pltpu.VMEM((4, LANES, LANES), F32),
            pltpu.VMEM((14, 2, LANES, LANES), F32),
            pltpu.VMEM((2, K, LANES), F32),
            pltpu.VMEM((2, K, LANES), F32),
        ],
        input_output_aliases={1: 4},
        compiler_params=params(),
        name="sketch",
    )(class_table, pt, xl, xr, yl, yr, rl, rr, ylo, yhi, cls2, w2, prior_block.astype(BF16), factor.astype(BF16))
    level_of, sibs = [], []
    if levels <= 2:
        for l in range(levels):
            for d in range(2**l):
                level_of.append(l)
                sibs.append(exchanged(v[l], "gy", 2**l + d))
    else:
        pending = v.astype(F32)
        for l in range(levels):
            got = exchanged(pending.astype(BF16), "gy", 2**l)
            level_of.append(l)
            sibs.append(got[0])
            pending = pending[1:] + got[1:].astype(F32)
    gx = pl.pallas_call(
        functools.partial(couple_kernel, K, tuple(level_of)),
        out_shape=shape((K, LANES), F32),
        in_specs=[VMEM] * (2 + len(sibs)),
        out_specs=VMEM,
        compiler_params=params(),
        name="couple",
    )(gx, u, *sibs)
    gx = summed(gx)
    basis, projected = pl.pallas_call(
        functools.partial(finish_kernel, K, NZ, X, cells),
        out_shape=(shape((K, NZ, X, W), F32), shape((K, K), F32)),
        in_specs=[VMEM] * 2,
        out_specs=(ANY, VMEM),
        scratch_shapes=[pltpu.VMEM((2, NZ, K * X, LANES), F32), pltpu.SemaphoreType.DMA((NZ, 2))],
        compiler_params=params(),
        name="finish",
    )(gx, s)
    return basis, projected


def solution(mesh):
    return jax.shard_map(
        shards,
        mesh=mesh,
        in_specs=(
            P(None, None, "gx", "gy"),
            P(None, "gx", "gy"),
            P(),
            P(None, "gx", "gy"),
            P("gy", None),
            P(None, None, "gy"),
            P(None, None, "gy"),
            P(),
        ),
        out_specs=(P(None, None, "gx", "gy"), P()),
        check_vma=False,
    )
```

```python
import functools
import jax
import jax.numpy as jnp
from jax import lax
from jax.experimental import pallas as pl
from jax.experimental.pallas import tpu as pltpu
from jax.sharding import PartitionSpec as P

HIGH = lax.Precision.HIGHEST
F32 = jnp.float32
BF16 = jnp.bfloat16
LANES = 128
SUB = 8
GROUP = 32
REACH = 3
AXES = ("gy", "gx")
UNROLL_ONE = 3
UNROLL_TWO = 2
UNROLL_GRAM = 8
NLINES = 4
GRAM_PARTS = 2
AUX = 16
VMEM = pl.BlockSpec(memory_space=pltpu.VMEM)
HBM = pl.BlockSpec(memory_space=pltpu.HBM)


def lanes_of(shape):
    return lax.broadcasted_iota(jnp.int32, shape, len(shape) - 1)


def halves(v):
    hi = v.astype(BF16)
    return hi, (v - hi.astype(F32)).astype(BF16)


def nt(a, b, precision=None):
    return lax.dot_general(a, b, (((1,), (1,)), ((), ())), precision=precision, preferred_element_type=F32)


def pack_kernel(K, NZ, X, p_hbm, cls_hbm, w_hbm, pt_ref, cg_ref, wg_ref, own_ref, y0_ref, y1_ref, x0_ref, x1_ref, p_ref, cls_ref, w_ref, edge, aux, yaux, sem):
    rows, ext = NZ * X, X + 4
    parts = 4
    step = K * rows // parts
    loads = [pltpu.make_async_copy(cls_hbm, cls_ref, sem.at[parts]), pltpu.make_async_copy(w_hbm, w_ref, sem.at[parts + 1])]
    for i in range(parts):
        loads.append(pltpu.make_async_copy(p_hbm.at[pl.ds(i * step, step)], p_ref.at[pl.ds(i * step, step)], sem.at[i]))
    for load in loads:
        load.start()
    loads[0].wait()
    loads[1].wait()
    odd = [lax.rem(lax.axis_index(axis), 2) for axis in ("gx", "gy")]
    turned = []
    for source, grid in ((cls_ref, cg_ref), (w_ref, wg_ref)):
        for h in range(2):
            grid[h] = jnp.zeros((LANES, LANES), F32)
        for z in range(NZ):
            v = source[z * X : (z + 1) * X, :].astype(F32)
            if source is cls_ref:
                v = v + 1.0
            at = z * GROUP + REACH
            for h in range(2):
                grid[h, at : at + X, :] = v[:, h * LANES : (h + 1) * LANES]
        turned.append(jnp.where(lanes_of((LANES, LANES)) < LANES // 2, grid[0], grid[1]).T)
    yaux[...] = jnp.zeros_like(yaux)
    for side in range(2):
        at = (0, 1, 2) if side == 0 else (LANES - 1, LANES - 2, LANES - 3)
        for d in range(3):
            yaux[side, d : d + 1, :] = turned[0][at[d] : at[d] + 1, :]
        w_hi, w_lo = halves(turned[1][at[0] : at[0] + 1, :])
        yaux[side, 3:4, :] = w_hi.astype(F32)
        yaux[side, 4:5, :] = w_lo.astype(F32)
    for i in range(parts):
        loads[2 + i].wait()
        for k in range(i * K // parts, (i + 1) * K // parts):
            v = p_ref[k * rows : (k + 1) * rows, :].astype(F32)
            for z in range(NZ):
                for h in range(2):
                    pt_ref[h, pl.ds((z * ext + 2) * K + k, X, stride=K), :] = v[z * X : (z + 1) * X, h * LANES : (h + 1) * LANES]
    lane = lanes_of((SUB, LANES))
    for kt in range(K // SUB):
        out = [jnp.zeros((SUB, LANES), F32) for _ in range(4)]
        for z in range(NZ):
            for x in range(X):
                row = (z * ext + 2 + x) * K + kt * SUB
                to = z * GROUP + x + REACH
                here = lane == to
                left, right = pt_ref[0, row : row + SUB, :], pt_ref[1, row : row + SUB, :]
                for i, (tile, col) in enumerate(((left, 0), (left, 1), (right, LANES - 1), (right, LANES - 2))):
                    out[i] = jnp.where(here, pltpu.roll(tile, (to - col) % LANES, 1), out[i])
        for i in range(4):
            edge[i, kt * SUB : (kt + 1) * SUB, :] = out[i]
        own_ref[0, kt * SUB : (kt + 1) * SUB, :] = out[0]
        own_ref[1, kt * SUB : (kt + 1) * SUB, :] = out[2]
    for m, ref in enumerate((y0_ref, y1_ref)):
        side = 1 - odd[1] if m == 0 else odd[1]
        for d in range(2):
            ref[d * K : (d + 1) * K, :] = edge[2 * side + d].astype(BF16)
        ref[2 * K : 2 * K + AUX, :] = yaux[side].astype(BF16)
    for m, ref in enumerate((x0_ref, x1_ref)):
        side = 1 - odd[0] if m == 0 else odd[0]
        for z in range(NZ):
            for i in range(2):
                row = pl.multiple_of((z * ext + 2 + side * (X - 2) + i) * K, SUB)
                for h in range(2):
                    ref[(z * 2 + i) * K : (z * 2 + i + 1) * K, h * LANES : (h + 1) * LANES] = pt_ref[h, pl.ds(row, K), :].astype(BF16)
        aux[...] = jnp.zeros_like(aux)
        for z in range(NZ):
            for d in range(3):
                aux[z * SUB + d : z * SUB + d + 1, :] = cls_ref[pl.ds(z * X + side * (X - 3) + d, 1), :].astype(F32) + 1.0
            w_hi, w_lo = halves(w_ref[pl.ds(z * X + side * (X - 1), 1), :])
            aux[z * SUB + 3 : z * SUB + 4, :] = w_hi.astype(F32)
            aux[z * SUB + 4 : z * SUB + 5, :] = w_lo.astype(F32)
        ref[2 * NZ * K : 2 * NZ * K + NZ * SUB, :] = aux[...].astype(BF16)


def merged(own, from_left, from_right):
    X = GROUP // 2
    m = lanes_of(own.shape) % GROUP
    left = pltpu.roll(from_left, LANES - X, 1)
    right = pltpu.roll(from_right, X, 1)
    out = jnp.where(m < X + REACH, own, jnp.where(m < X + 2 * REACH, right, 0.0))
    return jnp.where(m < REACH, left, out)


def main_kernel(
    K, NZ, X, levels, R,
    table_hbm, ranks_hbm, pt_in, x0_ref, x1_ref, y0_ref, y1_ref, q0_ref, q1_ref, own_ref, cin_ref, win_ref, left_hbm, right_hbm,
    s_ref, v_ref, u_ref, pt_ref, t_ref, cg, wg, rg, cf, hp, ht, ys, fac, table_ref, ranks_ref, sem,
):
    ext, wide = X + 4, X + 2
    KT = K // SUB
    sq = (LANES, LANES)
    lane_sq = lanes_of(sq)
    loads = [pltpu.make_async_copy(ref.at[pl.ds(0, levels)], fac.at[i], sem.at[i]) for i, ref in enumerate((right_hbm, left_hbm))]
    loads.append(pltpu.make_async_copy(table_hbm, table_ref, sem.at[2]))
    loads.append(pltpu.make_async_copy(ranks_hbm, ranks_ref, sem.at[3]))
    for load in loads:
        load.start()
    odd = [lax.rem(lax.axis_index(axis), 2) for axis in ("gx", "gy")]
    for m, ref in enumerate((x0_ref, x1_ref)):
        side = 1 - odd[0] if m == 0 else odd[0]
        for z in range(NZ):
            for i in range(2):
                at = pl.multiple_of((z * ext + i + side * (X + 2)) * K, SUB)
                for h in range(2):
                    cut = (slice((z * 2 + i) * K, (z * 2 + i + 1) * K), slice(h * LANES, (h + 1) * LANES))
                    pt_ref[h, pl.ds(at, K), :] = ref[cut].astype(F32)
    for m, ref in enumerate((y0_ref, y1_ref)):
        ys[0, 1 - odd[1] if m == 0 else odd[1]] = ref[...].astype(F32)
        for n, relay in enumerate((q0_ref, q1_ref)):
            ys[1 + (1 - odd[0] if n == 0 else odd[0]), 1 - odd[1] if m == 0 else odd[1]] = relay[m].astype(F32)
    for h in range(2):
        cg[1 + h] = cin_ref[h]
        wg[1 + h] = win_ref[h]
    for m, ref in enumerate((x0_ref, x1_ref)):
        side = 1 - odd[0] if m == 0 else odd[0]
        x_aux = ref[2 * NZ * K : 2 * NZ * K + NZ * SUB, :].astype(F32)
        for z in range(NZ):
            a = z * SUB
            for h in range(2):
                lo = slice(h * LANES, (h + 1) * LANES)
                for d in range(3):
                    cg[1 + h, pl.ds(z * GROUP + side * (X + REACH) + d, 1), :] = x_aux[a + d : a + d + 1, lo]
                beside = z * GROUP + REACH - 1 + side * (X + 1)
                wg[1 + h, pl.ds(beside, 1), :] = x_aux[a + 3 : a + 4, lo] + x_aux[a + 4 : a + 5, lo]
    spread = jnp.zeros(sq, F32)
    row_sq = lax.broadcasted_iota(jnp.int32, sq, 0)
    spread_w = jnp.zeros(sq, F32)
    for side in range(2):
        rows = merged(*(ys[n, side, 2 * K : 2 * K + AUX, :] for n in range(3)))
        at = (LANES - 1, LANES - 2, LANES - 3) if side == 0 else (0, 1, 2)
        for d in range(3):
            spread = jnp.where(row_sq == at[d], rows[d : d + 1, :], spread)
        spread_w = jnp.where(row_sq == at[0], rows[3:4, :] + rows[4:5, :], spread_w)
    y_class, y_weight = spread.T, spread_w.T
    keep = (lane_sq >= LANES // 2, lane_sq < LANES // 2)
    for side in range(2):
        cg[3 * side] = jnp.where(keep[side], y_class, 0.0)
        wg[3 * side] = jnp.where(keep[side], y_weight, 0.0)
    loads[2].wait()
    loads[3].wait()
    for t in range(4):
        ids = cg[t]
        cond = jnp.zeros(sq, F32)
        for j in range(table_ref.shape[0]):
            cond = jnp.where(ids == float(j + 1), table_ref[j], cond)
        cg[t] = cond

    zeros_g = jnp.zeros((GROUP, LANES), F32)

    def ahead(ref, t):
        nxt = ref[t + 1] if t < 3 else jnp.zeros(sq, F32)
        return jnp.where(lane_sq == LANES - 1, pltpu.roll(nxt, LANES - 1, 1), pltpu.roll(ref[t], LANES - 1, 1))

    def behind(ref, t):
        prv = ref[t - 1] if t > 0 else jnp.zeros(sq, F32)
        return jnp.where(lane_sq == 0, pltpu.roll(prv, 1, 1), pltpu.roll(ref[t], 1, 1))

    def around(ref, t):
        v = ref[t]
        return [
            pltpu.roll(v, LANES - 1, 0),
            pltpu.roll(v, 1, 0),
            ahead(ref, t),
            behind(ref, t),
            jnp.concatenate([v[GROUP:], zeros_g], 0),
            jnp.concatenate([zeros_g, v[:-GROUP]], 0),
        ]

    for t in range(4):
        c = cg[t]
        total = jnp.ones(sq, F32)
        for other in around(cg, t):
            total = total + 0.5 * (c + other)
        rg[t] = 1.0 / total
    picked = jnp.zeros(sq, F32)
    for t in range(4):
        c, r, w = cg[t], rg[t], wg[t]
        pairs = zip(around(cg, t), around(rg, t))
        terms = [r] + [0.5 * (c + c_n) * (r * r_n) for c_n, r_n in pairs]
        for j, term in enumerate(terms):
            if t in (1, 2):
                cf[j, t - 1] = w * term
                cf[7 + j, t - 1] = term
            else:
                to = j if t == 0 else 8 + j
                start = LANES - 1 if t == 0 else 0
                picked = jnp.where(lane_sq == to, pltpu.roll(w * term, (to - start) % LANES, 1), picked)
    edge_cf = picked.T
    for side in range(2):
        p1 = merged(*(ys[n, side, :K, :] for n in range(3)))
        p2 = ys[0, side, K : 2 * K, :]
        p0 = own_ref[side]
        y_next, y_prev = (p0, p2) if side == 0 else (p2, p0)
        parts = [
            p1,
            pltpu.roll(p1, LANES - 1, 1),
            pltpu.roll(p1, 1, 1),
            y_next,
            y_prev,
            pltpu.roll(p1, LANES - GROUP, 1),
            pltpu.roll(p1, GROUP, 1),
        ]
        total = edge_cf[8 * side : 8 * side + 1, :] * parts[0]
        for j in range(1, 7):
            total = total + edge_cf[8 * side + j : 8 * side + j + 1, :] * parts[j]
        hp[side] = p1
        ht[side] = total

    lane = lanes_of((SUB, LANES))
    is_first, is_last = lane == 0, lane == LANES - 1

    def stencil(z, coef_row, first_cf, src, centre_row, x_step, z_step, halo, kt):
        row = pl.multiple_of(centre_row + kt * SUB, SUB)
        c = [src[h, pl.ds(row, SUB), :] for h in range(2)]
        up = [src[h, pl.ds(row + x_step, SUB), :] for h in range(2)]
        down = [src[h, pl.ds(row - x_step, SUB), :] for h in range(2)]
        hl = pltpu.roll(halo[0, kt * SUB : (kt + 1) * SUB, :], LANES - coef_row, 1)
        hr = pltpu.roll(halo[1, kt * SUB : (kt + 1) * SUB, :], LANES - 1 - coef_row, 1)
        fwd = [pltpu.roll(v, LANES - 1, 1) for v in c]
        bwd = [pltpu.roll(v, 1, 1) for v in c]
        nxt = [jnp.where(is_last, fwd[1], fwd[0]), jnp.where(is_last, hr, fwd[1])]
        prv = [jnp.where(is_first, hl, bwd[0]), jnp.where(is_first, bwd[0], bwd[1])]
        out = []
        for h in range(2):
            co = [cf[first_cf + j, h, pl.ds(coef_row, 1), :] for j in range(7)]
            acc = co[0] * c[h] + co[1] * up[h] + co[2] * down[h] + co[3] * nxt[h] + co[4] * prv[h]
            if z < NZ - 1:
                acc = acc + co[5] * src[h, pl.ds(row + z_step, SUB), :]
            if z > 0:
                acc = acc + co[6] * src[h, pl.ds(row - z_step, SUB), :]
            out.append(acc)
        return row, out

    def stage_one(i, carry):
        for z in range(NZ):
            for kt in range(KT):
                _, out = stencil(z, z * GROUP + i + 2, 0, pt_ref, (z * ext + i + 1) * K, K, ext * K, hp, kt)
                to = pl.multiple_of((z * wide + i) * K + kt * SUB, SUB)
                for h in range(2):
                    t_ref[h, pl.ds(to, SUB), :] = out[h]
        return carry

    lax.fori_loop(0, wide, stage_one, 0, unroll=UNROLL_ONE)

    lane_k = lanes_of((K, LANES))
    loads[0].wait()
    loads[1].wait()
    rank = lax.broadcasted_iota(jnp.int32, (R, 1), 0)
    terms = []
    for l in range(levels):
        scale = float(2 * LANES * 2**l) ** -0.5
        terms.append(jnp.where(rank < ranks_ref[l], fac[0, l] * scale, 0.0))
    terms += [fac[1, l] for l in range(levels)]
    factor = jnp.concatenate(terms, 0).astype(BF16)

    def stage_two(i, carry):
        places = [[jnp.zeros((K, LANES), F32) for _ in range(levels)] for _ in range(2)]
        for half in range(2):
            x = 2 * i + half
            his = []
            for z in range(NZ):
                lines = []
                for kt in range(KT):
                    _, out = stencil(z, z * GROUP + x + REACH, 7, t_ref, (z * wide + x + 1) * K, K, wide * K, ht, kt)
                    row = pl.multiple_of((z * ext + x + 2) * K + kt * SUB, SUB)
                    to = pl.multiple_of((z * X + x) * K + kt * SUB, SUB)
                    both = []
                    for h in range(2):
                        s = out[h] + pt_ref[h, pl.ds(row, SUB), :]
                        s_ref[h, pl.ds(to, SUB), :] = s
                        both.append(s)
                    lines.append(jnp.concatenate(both, 1))
                his.append(jnp.concatenate(lines, 0).astype(BF16))
            coef = nt(jnp.concatenate(his, 0), factor)
            if coef.shape[1] < LANES:
                coef = jnp.concatenate([coef, jnp.zeros((NZ * K, LANES - coef.shape[1]), F32)], 1)
            for z in range(NZ):
                part = coef[z * K : (z + 1) * K]
                at = half * NZ * R + z * R
                here = (lane_k >= at) & (lane_k < at + R)
                for q in range(2):
                    for l in range(levels):
                        moved = pltpu.roll(part, (at - (q * levels + l) * R) % LANES, 1)
                        places[q][l] = jnp.where(here, moved, places[q][l])
        for l in range(levels):
            v_ref[l, i] = places[0][l].astype(BF16)
            u_ref[l, i] = places[1][l].astype(BF16)
        return carry

    lax.fori_loop(0, X // 2, stage_two, 0, unroll=UNROLL_TWO)


def gram_kernel(K, first, count, s_ref, block_ref, gx_ref):
    leaf_matrix = block_ref[...].astype(BF16)

    def chunk(i, carry):
        gram, mixed = carry
        his = []
        for n in range(NLINES):
            at = pl.multiple_of((first + i * NLINES + n) * K, SUB)
            hi, lo = halves(jnp.concatenate([s_ref[h, pl.ds(at, K), :] for h in range(2)], 1))
            gram = gram + nt(hi, jnp.concatenate([hi, lo], 0))
            his.append(hi)
        leaf = nt(jnp.concatenate(his, 0), leaf_matrix).astype(BF16)
        for n in range(NLINES):
            mixed = mixed + nt(his[n], leaf[n * K : (n + 1) * K])
        return gram, mixed

    init = (jnp.zeros((K, 2 * K), F32), jnp.zeros((K, K), F32))
    gram, mixed = lax.fori_loop(0, count // NLINES, chunk, init, unroll=UNROLL_GRAM)
    low = gram[:, K:]
    gx_ref[...] = jnp.zeros_like(gx_ref)
    gx_ref[:, :K] = gram[:, :K] + low + low.T
    gx_ref[:, LANES // 2 : LANES // 2 + K] = mixed


def couple_kernel(K, parts, u_ref, *refs):
    gx_refs, sib_refs, out_ref = refs[:parts], refs[parts:-1], refs[-1]
    total = jnp.zeros((K, K), F32)
    for l, ref in enumerate(sib_refs):
        for i in range(u_ref.shape[1]):
            total = total + nt(u_ref[l, i], ref[i])
    out_ref[...] = sum(ref[...] for ref in gx_refs)
    at = LANES // 2
    out_ref[:, at : at + K] = out_ref[:, at : at + K] + total


def finish_kernel(K, NZ, X, cells, gx_ref, s_ref, basis_ref, proj_ref, out, sem):
    lane = lanes_of((K, LANES))
    row = lax.broadcasted_iota(jnp.int32, (K, LANES), 0)
    half = LANES // 2
    gx = gx_ref[...] * (1.0 / cells)
    gram = gx[:, :K]
    mixed = gram + gx[:, half : half + K]
    aug = jnp.where(lane < K, gx, jnp.where(lane - half == row, 1.0, 0.0))
    for j in range(K - 1):
        pivot_row = aug[j : j + 1, :]
        factor = aug[:, j : j + 1] * (1.0 / aug[j : j + 1, j : j + 1])
        aug = aug - jnp.where(row > j, factor, 0.0) * pivot_row
    pivots = jnp.sum(jnp.where(lane == row, aug, 0.0), axis=1, keepdims=True)
    inverse = aug[:, half : half + K] * lax.rsqrt(pivots)
    left = jnp.dot(inverse, mixed, precision=HIGH, preferred_element_type=F32)
    proj_ref[...] = nt(left, inverse, precision=HIGH)
    i_hi, i_lo = halves(inverse)
    lhs = jnp.concatenate([i_hi, i_lo, i_hi], 1)
    W = 2 * LANES
    copies = []
    for z in range(NZ):

        def line(x, carry, z=z):
            at = pl.multiple_of((z * X + x) * K, SUB)
            s = jnp.concatenate([s_ref[h, pl.ds(at, K), :] for h in range(2)], 1)
            hi, lo = halves(s)
            b = jnp.dot(lhs, jnp.concatenate([hi, hi, lo], 0), preferred_element_type=F32)
            for h in range(2):
                out[h, z, pl.ds(x, K, stride=X), :] = b[:, h * LANES : (h + 1) * LANES]
            return carry

        lax.fori_loop(0, X, line, 0, unroll=True)
        for h in range(2):
            for part in range(1):
                copies.append(
                    pltpu.make_async_copy(
                        out.at[h, z].reshape(K, X, LANES), basis_ref.at[:, z, :, pl.ds(h * LANES, LANES)], sem.at[z, h]
                    )
                )
                copies[-1].start()
    for c in copies:
        c.wait()


def in_hbm(v):
    return pltpu.with_memory_space_constraint(v, pltpu.HBM)


def exchanged(v, axis, bits):
    return lax.ppermute(v, axis, [(i, i ^ bits) for i in range(lax.axis_size(axis))])


def paired(v, axis, first):
    n = lax.axis_size(axis)
    swaps = [(i, i + 1) for i in range(first, n - 1, 2)]
    return lax.ppermute(v, axis, swaps + [(j, i) for i, j in swaps])


def summed(v):
    for axis in AXES:
        bit = 1
        while bit < lax.axis_size(axis):
            v = v + exchanged(v, axis, bit)
            bit *= 2
    return v


def shards(probes, classes, class_table, weights, prior_block, prior_left, prior_right, block_ranks):
    K, NZ, X, W = probes.shape
    R = prior_left.shape[1]
    levels = lax.axis_size("gy").bit_length() - 1
    cells = float(NZ * X * W * lax.axis_size("gx") * lax.axis_size("gy"))
    rows, ext, wide = NZ * X, X + 4, X + 2
    shape = jax.ShapeDtypeStruct
    cls2, w2 = classes.reshape(rows, W), weights.reshape(rows, W)
    params = functools.partial(pltpu.CompilerParams, vmem_limit_bytes=32 << 20)
    y_rows, x_rows = 2 * K + AUX, 2 * NZ * K + NZ * SUB
    square = (LANES, LANES)
    pt, cg, wg, own, y0, y1, x0, x1 = pl.pallas_call(
        functools.partial(pack_kernel, K, NZ, X),
        out_shape=(
            shape((2, NZ * ext * K, LANES), F32),
            shape((2, *square), F32),
            shape((2, *square), F32),
            shape((2, K, LANES), F32),
            shape((y_rows, LANES), BF16),
            shape((y_rows, LANES), BF16),
            shape((x_rows, W), BF16),
            shape((x_rows, W), BF16),
        ),
        in_specs=[HBM] * 3,
        out_specs=(VMEM,) * 8,
        scratch_shapes=[
            pltpu.VMEM((K * rows, W), BF16),
            pltpu.VMEM((rows, W), jnp.int32),
            pltpu.VMEM((rows, W), F32),
            pltpu.VMEM((4, K, LANES), F32),
            pltpu.VMEM((NZ * SUB, W), F32),
            pltpu.VMEM((2, AUX, LANES), F32),
            pltpu.SemaphoreType.DMA((6,)),
        ],
        compiler_params=params(),
        name="pack",
    )(in_hbm(probes.reshape(K * rows, W)), in_hbm(cls2), in_hbm(w2))
    y0, y1 = paired(y0, "gy", 0), paired(y1, "gy", 1)
    x0, x1 = paired(x0, "gx", 0), paired(x1, "gx", 1)
    both = jnp.stack([y0, y1])
    q0, q1 = paired(both, "gx", 0), paired(both, "gx", 1)
    slab = (2, rows * K, LANES)
    side = (levels, X // 2, K, LANES)
    s, v, u, _ = pl.pallas_call(
        functools.partial(main_kernel, K, NZ, X, levels, R),
        out_shape=(shape(slab, F32), shape(side, BF16), shape(side, BF16), shape(pt.shape, F32)),
        in_specs=[HBM] * 2 + [VMEM] * 10 + [HBM] * 2,
        out_specs=(VMEM,) * 4,
        scratch_shapes=[
            pltpu.VMEM((2, NZ * wide * K, LANES), F32),
            pltpu.VMEM((4, *square), F32),
            pltpu.VMEM((4, *square), F32),
            pltpu.VMEM((4, *square), F32),
            pltpu.VMEM((14, 2, *square), F32),
            pltpu.VMEM((2, K, LANES), F32),
            pltpu.VMEM((2, K, LANES), F32),
            pltpu.VMEM((3, 2, y_rows, LANES), F32),
            pltpu.VMEM((2, levels, R, W), F32),
            pltpu.SMEM(class_table.shape, F32),
            pltpu.SMEM(block_ranks.shape, jnp.int32),
            pltpu.SemaphoreType.DMA((4,)),
        ],
        input_output_aliases={2: 3},
        compiler_params=params(),
        name="sketch",
    )(in_hbm(class_table), in_hbm(block_ranks), pt, x0, x1, y0, y1, q0, q1, own, cg, wg, in_hbm(prior_left), in_hbm(prior_right))
    share = rows // GRAM_PARTS
    parts = []
    for i in range(GRAM_PARTS):
        parts.append(
            pl.pallas_call(
                functools.partial(gram_kernel, K, i * share, share),
                out_shape=shape((K, LANES), F32),
                in_specs=[VMEM] * 2,
                out_specs=VMEM,
                cost_estimate=pl.CostEstimate(flops=2 * 300 * K * share * W, bytes_accessed=8 << 20, transcendentals=0),
                compiler_params=params(),
                name=f"gram_{i}",
            )(s, prior_block)
        )
    sibs = []
    pending = v
    for l in range(levels):
        got = exchanged(pending, "gy", 2**l)
        sibs.append(got[0])
        pending = (pending[1:].astype(F32) + got[1:].astype(F32)).astype(BF16)
    gx = pl.pallas_call(
        functools.partial(couple_kernel, K, GRAM_PARTS),
        out_shape=shape((K, LANES), F32),
        in_specs=[VMEM] * (1 + GRAM_PARTS + levels),
        out_specs=VMEM,
        compiler_params=params(),
        name="couple",
    )(u, *parts, *sibs)
    gx = summed(gx)
    basis, projected = pl.pallas_call(
        functools.partial(finish_kernel, K, NZ, X, cells),
        out_shape=(shape((K, NZ, X, W), F32), shape((K, K), F32)),
        in_specs=[VMEM] * 2,
        out_specs=(HBM, VMEM),
        scratch_shapes=[pltpu.VMEM((2, NZ, K * X, LANES), F32), pltpu.SemaphoreType.DMA((NZ, 2))],
        compiler_params=params(),
        name="finish",
    )(gx, s)
    return basis, projected


def solution(mesh):
    return jax.shard_map(
        shards,
        mesh=mesh,
        in_specs=(
            P(None, None, "gx", "gy"),
            P(None, "gx", "gy"),
            P(),
            P(None, "gx", "gy"),
            P("gy", None),
            P(None, None, "gy"),
            P(None, None, "gy"),
            P(),
        ),
        out_specs=(P(None, None, "gx", "gy"), P()),
        check_vma=False,
    )
```

```python
import functools
import jax
import jax.numpy as jnp
from jax import lax
from jax.experimental import pallas as pl
from jax.experimental.pallas import tpu as pltpu
from jax.sharding import PartitionSpec as P

HIGH = lax.Precision.HIGHEST
F32 = jnp.float32
BF16 = jnp.bfloat16
LANES = 128
SUB = 8
GROUP = 32
REACH = 3
AXES = ("gy", "gx")
UNROLL_ONE = 3
UNROLL_TWO = 2
UNROLL_GRAM = 8
NLINES = 4
GRAM_PARTS = 2
AUX = 16
VMEM = pl.BlockSpec(memory_space=pltpu.VMEM)
HBM = pl.BlockSpec(memory_space=pltpu.HBM)


def lanes_of(shape):
    return lax.broadcasted_iota(jnp.int32, shape, len(shape) - 1)


def halves(v):
    hi = v.astype(BF16)
    return hi, (v - hi.astype(F32)).astype(BF16)


def nt(a, b, precision=None):
    return lax.dot_general(a, b, (((1,), (1,)), ((), ())), precision=precision, preferred_element_type=F32)


def pack_kernel(K, NZ, X, p_hbm, cls_hbm, w_hbm, pt_ref, cg_ref, wg_ref, own_ref, y0_ref, y1_ref, p_ref, cls_ref, w_ref, edge, yaux, sem):
    rows, ext = NZ * X, X + 4
    parts = 4
    step = K * rows // parts
    loads = [pltpu.make_async_copy(cls_hbm, cls_ref, sem.at[parts]), pltpu.make_async_copy(w_hbm, w_ref, sem.at[parts + 1])]
    for i in range(parts):
        loads.append(pltpu.make_async_copy(p_hbm.at[pl.ds(i * step, step)], p_ref.at[pl.ds(i * step, step)], sem.at[i]))
    for load in loads:
        load.start()
    loads[0].wait()
    loads[1].wait()
    odd = lax.rem(lax.axis_index("gy"), 2)
    turned = []
    for source, grid in ((cls_ref, cg_ref), (w_ref, wg_ref)):
        for h in range(2):
            grid[h] = jnp.zeros((LANES, LANES), F32)
        for z in range(NZ):
            v = source[z * X : (z + 1) * X, :].astype(F32)
            if source is cls_ref:
                v = v + 1.0
            at = z * GROUP + REACH
            for h in range(2):
                grid[h, at : at + X, :] = v[:, h * LANES : (h + 1) * LANES]
        turned.append(jnp.where(lanes_of((LANES, LANES)) < LANES // 2, grid[0], grid[1]).T)
    yaux[...] = jnp.zeros_like(yaux)
    for side in range(2):
        at = (0, 1, 2) if side == 0 else (LANES - 1, LANES - 2, LANES - 3)
        for d in range(3):
            yaux[side, d : d + 1, :] = turned[0][at[d] : at[d] + 1, :]
        w_hi, w_lo = halves(turned[1][at[0] : at[0] + 1, :])
        yaux[side, 3:4, :] = w_hi.astype(F32)
        yaux[side, 4:5, :] = w_lo.astype(F32)
    for i in range(parts):
        loads[2 + i].wait()
        for k in range(i * K // parts, (i + 1) * K // parts):
            v = p_ref[k * rows : (k + 1) * rows, :].astype(F32)
            for z in range(NZ):
                for h in range(2):
                    pt_ref[h, pl.ds((z * ext + 2) * K + k, X, stride=K), :] = v[z * X : (z + 1) * X, h * LANES : (h + 1) * LANES]
    lane = lanes_of((SUB, LANES))
    for kt in range(K // SUB):
        out = [jnp.zeros((SUB, LANES), F32) for _ in range(4)]
        for z in range(NZ):
            for x in range(X):
                row = (z * ext + 2 + x) * K + kt * SUB
                to = z * GROUP + x + REACH
                here = lane == to
                left, right = pt_ref[0, row : row + SUB, :], pt_ref[1, row : row + SUB, :]
                for i, (tile, col) in enumerate(((left, 0), (left, 1), (right, LANES - 1), (right, LANES - 2))):
                    out[i] = jnp.where(here, pltpu.roll(tile, (to - col) % LANES, 1), out[i])
        for i in range(4):
            edge[i, kt * SUB : (kt + 1) * SUB, :] = out[i]
        own_ref[0, kt * SUB : (kt + 1) * SUB, :] = out[0]
        own_ref[1, kt * SUB : (kt + 1) * SUB, :] = out[2]
    for m, ref in enumerate((y0_ref, y1_ref)):
        side = side_of(m, odd)
        for d in range(2):
            ref[d * K : (d + 1) * K, :] = edge[2 * side + d].astype(BF16)
        ref[2 * K : 2 * K + AUX, :] = yaux[side].astype(BF16)


def side_of(m, odd):
    return 1 - odd if m == 0 else odd


def send_kernel(K, NZ, X, pt_ref, cg_ref, wg_ref, y0_ref, y1_ref, q0_ref, q1_ref, x0_ref, x1_ref, aux):
    ext = X + 4
    odd = lax.rem(lax.axis_index("gx"), 2)
    for m, ref in enumerate((q0_ref, q1_ref)):
        side = side_of(m, odd)
        for n, got in enumerate((y0_ref, y1_ref)):
            at = n * (K + AUX)
            ref[at : at + K, :] = got[:K, :]
            ref[at + K : at + K + AUX, :] = got[2 * K : 2 * K + AUX, :]
        aux[...] = jnp.zeros_like(aux)
        for h in range(2):
            for z in range(NZ):
                to = (h * NZ + z) * SUB
                for d in range(3):
                    aux[to + d : to + d + 1, :] = cg_ref[h, pl.ds(z * GROUP + REACH + side * (X - 3) + d, 1), :]
                w_hi, w_lo = halves(wg_ref[h, pl.ds(z * GROUP + REACH + side * (X - 1), 1), :])
                aux[to + 3 : to + 4, :] = w_hi.astype(F32)
                aux[to + 4 : to + 5, :] = w_lo.astype(F32)
        ref[2 * (K + AUX) :, :] = aux[...].astype(BF16)
    for m, ref in enumerate((x0_ref, x1_ref)):
        side = side_of(m, odd)
        for z in range(NZ):
            for i in range(2):
                row = pl.multiple_of((z * ext + 2 + side * (X - 2) + i) * K, SUB)
                for h in range(2):
                    ref[(z * 2 + i) * K : (z * 2 + i + 1) * K, h * LANES : (h + 1) * LANES] = pt_ref[h, pl.ds(row, K), :].astype(BF16)


def prep_kernel(levels, R, after_ref, ranks_ref, right_ref, left_ref, fr_ref, fl_ref):
    del after_ref
    rank = lax.broadcasted_iota(jnp.int32, (R, 1), 0)
    per = fr_ref.shape[0]
    fr_ref[...] = jnp.zeros_like(fr_ref)
    fl_ref[...] = jnp.zeros_like(fl_ref)
    for l in range(levels):
        scale = float(2 * LANES * 2**l) ** -0.5
        right = jnp.where(rank < ranks_ref[l], right_ref[l] * scale, 0.0).astype(BF16)
        left = left_ref[l].astype(BF16)
        for i in range(per):
            at = l * LANES + i * R
            fr_ref[i, at : at + R, :] = right
            fl_ref[i, at : at + R, :] = left


def mult(v):
    return v if isinstance(v, int) else pl.multiple_of(v, SUB)


def stencil(NZ, z, coef_row, cf, first_cf, src, centre_row, x_step, z_step, halo, kt):
    lane = lanes_of((SUB, LANES))
    is_first, is_last = lane == 0, lane == LANES - 1

    def at(row):
        return pl.ds(mult(row), SUB)

    row = centre_row + kt * SUB
    c = [src[h, at(row), :] for h in range(2)]
    up = [src[h, at(row + x_step), :] for h in range(2)]
    down = [src[h, at(row - x_step), :] for h in range(2)]
    hl = pltpu.roll(halo[0, kt * SUB : (kt + 1) * SUB, :], LANES - coef_row, 1)
    hr = pltpu.roll(halo[1, kt * SUB : (kt + 1) * SUB, :], LANES - 1 - coef_row, 1)
    fwd = [pltpu.roll(v, LANES - 1, 1) for v in c]
    bwd = [pltpu.roll(v, 1, 1) for v in c]
    nxt = [jnp.where(is_last, fwd[1], fwd[0]), jnp.where(is_last, hr, fwd[1])]
    prv = [jnp.where(is_first, hl, bwd[0]), jnp.where(is_first, bwd[0], bwd[1])]
    out = []
    for h in range(2):
        co = [cf[first_cf + j, h, pl.ds(coef_row, 1), :] for j in range(7)]
        acc = co[0] * c[h] + co[1] * up[h] + co[2] * down[h] + co[3] * nxt[h] + co[4] * prv[h]
        if z < NZ - 1:
            acc = acc + co[5] * src[h, at(row + z_step), :]
        if z > 0:
            acc = acc + co[6] * src[h, at(row - z_step), :]
        out.append(acc)
    return out


def stage_one(K, NZ, X, x, cf, pt_ref, t_ref, hp):
    ext, wide = X + 4, X + 2
    for z in range(NZ):
        for kt in range(K // SUB):
            out = stencil(NZ, z, z * GROUP + x + REACH, cf, 0, pt_ref, (z * ext + x + 2) * K, K, ext * K, hp, kt)
            to = mult((z * wide + x + 1) * K + kt * SUB)
            for h in range(2):
                t_ref[h, pl.ds(to, SUB), :] = out[h]


def stage_two(K, NZ, X, x, cf, pt_ref, t_ref, s_ref, ht):
    ext, wide = X + 4, X + 2
    his = []
    for z in range(NZ):
        lines = []
        for kt in range(K // SUB):
            out = stencil(NZ, z, z * GROUP + x + REACH, cf, 7, t_ref, (z * wide + x + 1) * K, K, wide * K, ht, kt)
            row = mult((z * ext + x + 2) * K + kt * SUB)
            to = mult((z * X + x) * K + kt * SUB)
            both = []
            for h in range(2):
                s = out[h] + pt_ref[h, pl.ds(row, SUB), :]
                s_ref[h, pl.ds(to, SUB), :] = s
                both.append(s)
            lines.append(jnp.concatenate(both, 1))
        his.append(jnp.concatenate(lines, 0).astype(BF16))
    return jnp.concatenate(his, 0)


def merged(own, from_left, from_right):
    X = GROUP // 2
    m = lanes_of(own.shape) % GROUP
    left = pltpu.roll(from_left, LANES - X, 1)
    right = pltpu.roll(from_right, X, 1)
    out = jnp.where(m < X + REACH, own, jnp.where(m < X + 2 * REACH, right, 0.0))
    return jnp.where(m < REACH, left, out)


def inner_kernel(
    K, NZ, X, R,
    table_hbm, pt_ref, y0_ref, y1_ref, q0_ref, q1_ref, own_ref, cin_ref, win_ref, fr_ref,
    s_ref, t_ref, cf, hp, ht, acc_ref, cg, wg, rg, ys, xs, table_ref, sem,
):
    sq = (LANES, LANES)
    lane_sq = lanes_of(sq)
    load = pltpu.make_async_copy(table_hbm, table_ref, sem)
    load.start()
    place = [lax.axis_index(axis) for axis in ("gx", "gy")]
    last = [lax.axis_size(axis) - 1 for axis in ("gx", "gy")]
    odd = [lax.rem(v, 2) for v in place]

    def there(axis, side):
        edge = lax.select(side == 0, place[axis], last[axis] - place[axis])
        return lax.select(edge > 0, jnp.float32(1.0), jnp.float32(0.0))

    for m, ref in enumerate((y0_ref, y1_ref)):
        side = side_of(m, odd[1])
        y_there = there(1, side)
        ys[0, side] = ref[...].astype(F32) * y_there
        for n, relay in enumerate((q0_ref, q1_ref)):
            x_side = side_of(n, odd[0])
            factor = y_there * there(0, x_side)
            at = m * (K + AUX)
            ys[1 + x_side, side, :K, :] = relay[at : at + K, :].astype(F32) * factor
            ys[1 + x_side, side, 2 * K :, :] = relay[at + K : at + K + AUX, :].astype(F32) * factor
    for n, relay in enumerate((q0_ref, q1_ref)):
        x_side = side_of(n, odd[0])
        xs[x_side] = relay[2 * (K + AUX) :, :].astype(F32) * there(0, x_side)
    for h in range(2):
        cg[1 + h] = cin_ref[h]
        wg[1 + h] = win_ref[h]
    for side in range(2):
        for z in range(NZ):
            for h in range(2):
                a = (h * NZ + z) * SUB
                start = z * GROUP + side * (X + REACH)
                cg[1 + h, start : start + REACH, :] = xs[side, a : a + REACH, :]
                beside = z * GROUP + REACH - 1 + side * (X + 1)
                wg[1 + h, beside : beside + 1, :] = xs[side, a + 3 : a + 4, :] + xs[side, a + 4 : a + 5, :]
    spread = jnp.zeros(sq, F32)
    row_sq = lax.broadcasted_iota(jnp.int32, sq, 0)
    spread_w = jnp.zeros(sq, F32)
    for side in range(2):
        rows = merged(*(ys[n, side, 2 * K : 2 * K + AUX, :] for n in range(3)))
        at = (LANES - 1, LANES - 2, LANES - 3) if side == 0 else (0, 1, 2)
        for d in range(3):
            spread = jnp.where(row_sq == at[d], rows[d : d + 1, :], spread)
        spread_w = jnp.where(row_sq == at[0], rows[3:4, :] + rows[4:5, :], spread_w)
    y_class, y_weight = spread.T, spread_w.T
    keep = (lane_sq >= LANES // 2, lane_sq < LANES // 2)
    for side in range(2):
        cg[3 * side] = jnp.where(keep[side], y_class, 0.0)
        wg[3 * side] = jnp.where(keep[side], y_weight, 0.0)
    load.wait()
    for t in range(4):
        ids = cg[t]
        cond = jnp.zeros(sq, F32)
        for j in range(table_ref.shape[0]):
            cond = jnp.where(ids == float(j + 1), table_ref[j], cond)
        cg[t] = cond

    zeros_g = jnp.zeros((GROUP, LANES), F32)

    def ahead(ref, t):
        nxt = ref[t + 1] if t < 3 else jnp.zeros(sq, F32)
        return jnp.where(lane_sq == LANES - 1, pltpu.roll(nxt, LANES - 1, 1), pltpu.roll(ref[t], LANES - 1, 1))

    def behind(ref, t):
        prv = ref[t - 1] if t > 0 else jnp.zeros(sq, F32)
        return jnp.where(lane_sq == 0, pltpu.roll(prv, 1, 1), pltpu.roll(ref[t], 1, 1))

    def around(ref, t):
        v = ref[t]
        return [
            pltpu.roll(v, LANES - 1, 0),
            pltpu.roll(v, 1, 0),
            ahead(ref, t),
            behind(ref, t),
            jnp.concatenate([v[GROUP:], zeros_g], 0),
            jnp.concatenate([zeros_g, v[:-GROUP]], 0),
        ]

    for t in range(4):
        c = cg[t]
        total = jnp.ones(sq, F32)
        for other in around(cg, t):
            total = total + 0.5 * (c + other)
        rg[t] = 1.0 / total
    picked = jnp.zeros(sq, F32)
    for t in range(4):
        c, r, w = cg[t], rg[t], wg[t]
        pairs = zip(around(cg, t), around(rg, t))
        terms = [r] + [0.5 * (c + c_n) * (r * r_n) for c_n, r_n in pairs]
        for j, term in enumerate(terms):
            if t in (1, 2):
                cf[j, t - 1] = w * term
                cf[7 + j, t - 1] = term
            else:
                to = j if t == 0 else 8 + j
                start = LANES - 1 if t == 0 else 0
                picked = jnp.where(lane_sq == to, pltpu.roll(w * term, (to - start) % LANES, 1), picked)
    edge_cf = picked.T
    for side in range(2):
        p1 = merged(*(ys[n, side, :K, :] for n in range(3)))
        p2 = ys[0, side, K : 2 * K, :]
        p0 = own_ref[side]
        y_next, y_prev = (p0, p2) if side == 0 else (p2, p0)
        parts = [
            p1,
            pltpu.roll(p1, LANES - 1, 1),
            pltpu.roll(p1, 1, 1),
            y_next,
            y_prev,
            pltpu.roll(p1, LANES - GROUP, 1),
            pltpu.roll(p1, GROUP, 1),
        ]
        total = edge_cf[8 * side : 8 * side + 1, :] * parts[0]
        for j in range(1, 7):
            total = total + edge_cf[8 * side + j : 8 * side + j + 1, :] * parts[j]
        hp[side] = p1
        ht[side] = total


    def first_lines(i, carry):
        stage_one(K, NZ, X, i, cf, pt_ref, t_ref, hp)
        return carry

    lax.fori_loop(1, X - 1, first_lines, 0, unroll=UNROLL_ONE)
    acc_ref[...] = jnp.zeros_like(acc_ref)
    per = LANES // R // 2

    def second_lines(i, carry):
        for half in range(2):
            lines = stage_two(K, NZ, X, 2 * i + half, cf, pt_ref, t_ref, s_ref, ht)
            group = lax.div(i, per)
            acc_ref[group] = acc_ref[group] + nt(lines, fr_ref[2 * lax.rem(i, per) + half])
        return carry

    lax.fori_loop(1, X // 2 - 1, second_lines, 0, unroll=UNROLL_TWO)


def edge_kernel(K, NZ, X, R, pt_in, t_in, s_in, x0_ref, x1_ref, cf, hp, ht, acc_ref, fr_ref, pt_ref, t_ref, s_ref, v_ref):
    ext = X + 4
    odd = lax.rem(lax.axis_index("gx"), 2)
    for m, ref in enumerate((x0_ref, x1_ref)):
        side = side_of(m, odd)
        for z in range(NZ):
            for i in range(2):
                at = pl.multiple_of((z * ext + i + side * (X + 2)) * K, SUB)
                for h in range(2):
                    cut = (slice((z * 2 + i) * K, (z * 2 + i + 1) * K), slice(h * LANES, (h + 1) * LANES))
                    pt_ref[h, pl.ds(at, K), :] = ref[cut].astype(F32)
    for x in (-1, 0, X - 1, X):
        stage_one(K, NZ, X, x, cf, pt_ref, t_ref, hp)
    per = LANES // R
    sums = [acc_ref[g] for g in range(X // per)]
    for x in (0, 1, X - 2, X - 1):
        lines = stage_two(K, NZ, X, x, cf, pt_ref, t_ref, s_ref, ht)
        sums[x // per] = sums[x // per] + nt(lines, fr_ref[x % per])
    for g, total in enumerate(sums):
        for l in range(v_ref.shape[0]):
            v_ref[l, g] = total[:, l * LANES : (l + 1) * LANES].astype(BF16)


def left_kernel(K, NZ, X, R, after_ref, s_ref, fl_ref, u_ref):
    del after_ref
    per = LANES // R
    for g in range(X // per):
        total = None
        for i in range(per):
            x = g * per + i
            lines = []
            for z in range(NZ):
                at = (z * X + x) * K
                lines.append(jnp.concatenate([s_ref[h, at : at + K, :] for h in range(2)], 1).astype(BF16))
            term = nt(jnp.concatenate(lines, 0), fl_ref[i])
            total = term if total is None else total + term
        for l in range(u_ref.shape[0]):
            u_ref[l, g] = total[:, l * LANES : (l + 1) * LANES].astype(BF16)


def gram_kernel(K, first, count, s_ref, block_ref, *refs):
    gx_ref = refs[-1]
    leaf_matrix = block_ref[...].astype(BF16)

    def chunk(i, carry):
        gram, mixed = carry
        his = []
        for n in range(NLINES):
            at = pl.multiple_of((first + i * NLINES + n) * K, SUB)
            hi, lo = halves(jnp.concatenate([s_ref[h, pl.ds(at, K), :] for h in range(2)], 1))
            gram = gram + nt(hi, jnp.concatenate([hi, lo], 0))
            his.append(hi)
        leaf = nt(jnp.concatenate(his, 0), leaf_matrix).astype(BF16)
        for n in range(NLINES):
            mixed = mixed + nt(his[n], leaf[n * K : (n + 1) * K])
        return gram, mixed

    init = (jnp.zeros((K, 2 * K), F32), jnp.zeros((K, K), F32))
    gram, mixed = lax.fori_loop(0, count // NLINES, chunk, init, unroll=UNROLL_GRAM)
    low = gram[:, K:]
    gx_ref[...] = jnp.zeros_like(gx_ref)
    gx_ref[:, :K] = gram[:, :K] + low + low.T
    gx_ref[:, LANES // 2 : LANES // 2 + K] = mixed


def couple_kernel(K, parts, u_ref, *refs):
    gx_refs, sib_refs, out_ref = refs[:parts], refs[parts:-1], refs[-1]
    total = jnp.zeros((K, K), F32)
    for l, ref in enumerate(sib_refs):
        for g in range(u_ref.shape[1]):
            for at in range(0, u_ref.shape[2], K):
                total = total + nt(u_ref[l, g, at : at + K, :], ref[g, at : at + K, :])
    out_ref[...] = sum(ref[...] for ref in gx_refs)
    at = LANES // 2
    out_ref[:, at : at + K] = out_ref[:, at : at + K] + total


def finish_kernel(K, NZ, X, cells, gx_ref, s_ref, basis_ref, proj_ref, out, sem):
    lane = lanes_of((K, LANES))
    row = lax.broadcasted_iota(jnp.int32, (K, LANES), 0)
    half = LANES // 2
    gx = gx_ref[...] * (1.0 / cells)
    gram = gx[:, :K]
    mixed = gram + gx[:, half : half + K]
    aug = jnp.where(lane < K, gx, jnp.where(lane - half == row, 1.0, 0.0))
    for j in range(K - 1):
        pivot_row = aug[j : j + 1, :]
        factor = aug[:, j : j + 1] * (1.0 / aug[j : j + 1, j : j + 1])
        aug = aug - jnp.where(row > j, factor, 0.0) * pivot_row
    pivots = jnp.sum(jnp.where(lane == row, aug, 0.0), axis=1, keepdims=True)
    inverse = aug[:, half : half + K] * lax.rsqrt(pivots)
    left = jnp.dot(inverse, mixed, precision=HIGH, preferred_element_type=F32)
    proj_ref[...] = nt(left, inverse, precision=HIGH)
    i_hi, i_lo = halves(inverse)
    lhs = jnp.concatenate([i_hi, i_lo, i_hi], 1)
    copies = []
    for z in range(NZ):

        def line(x, carry, z=z):
            at = pl.multiple_of((z * X + x) * K, SUB)
            s = jnp.concatenate([s_ref[h, pl.ds(at, K), :] for h in range(2)], 1)
            hi, lo = halves(s)
            b = jnp.dot(lhs, jnp.concatenate([hi, hi, lo], 0), preferred_element_type=F32)
            for h in range(2):
                out[h, z, pl.ds(x, K, stride=X), :] = b[:, h * LANES : (h + 1) * LANES]
            return carry

        lax.fori_loop(0, X, line, 0, unroll=True)
        for h in range(2):
            for _ in range(1):
                copies.append(
                    pltpu.make_async_copy(
                        out.at[h, z].reshape(K, X, LANES), basis_ref.at[:, z, :, pl.ds(h * LANES, LANES)], sem.at[z, h]
                    )
                )
                copies[-1].start()
    for c in copies:
        c.wait()


def in_hbm(v):
    return pltpu.with_memory_space_constraint(v, pltpu.HBM)


def exchanged(v, axis, bits):
    return lax.ppermute(v, axis, [(i, i ^ bits) for i in range(lax.axis_size(axis))])


def paired(v, axis, first, ring=True):
    n = lax.axis_size(axis)
    swaps = [(i, i + 1) for i in range(first, n - 1, 2)]
    if first and ring:
        swaps = swaps + [(0, n - 1)]
    return lax.ppermute(v, axis, swaps + [(j, i) for i, j in swaps])


def summed(v):
    for axis in AXES:
        bit = 1
        while bit < lax.axis_size(axis):
            v = v + exchanged(v, axis, bit)
            bit *= 2
    return v


def shards(probes, classes, class_table, weights, prior_block, prior_left, prior_right, block_ranks):
    K, NZ, X, W = probes.shape
    R = prior_left.shape[1]
    levels = lax.axis_size("gy").bit_length() - 1
    cells = float(NZ * X * W * lax.axis_size("gx") * lax.axis_size("gy"))
    rows, ext, wide = NZ * X, X + 4, X + 2
    shape = jax.ShapeDtypeStruct
    cls2, w2 = classes.reshape(rows, W), weights.reshape(rows, W)
    params = functools.partial(pltpu.CompilerParams, vmem_limit_bytes=32 << 20)
    y_rows, x_rows = 2 * K + AUX, 2 * NZ * K
    q_rows = 2 * (K + AUX) + 2 * NZ * SUB
    square = (LANES, LANES)
    per = LANES // R
    groups = X // per

    def cost(flops, nbytes=4 << 20):
        return pl.CostEstimate(flops=flops, bytes_accessed=nbytes, transcendentals=0)

    pt, cg, wg, own, y0, y1 = pl.pallas_call(
        functools.partial(pack_kernel, K, NZ, X),
        out_shape=(
            shape((2, NZ * ext * K, LANES), F32),
            shape((2, *square), F32),
            shape((2, *square), F32),
            shape((2, K, LANES), F32),
            shape((y_rows, LANES), BF16),
            shape((y_rows, LANES), BF16),
        ),
        in_specs=[HBM] * 3,
        out_specs=(VMEM,) * 6,
        scratch_shapes=[
            pltpu.VMEM((K * rows, W), BF16),
            pltpu.VMEM((rows, W), jnp.int32),
            pltpu.VMEM((rows, W), F32),
            pltpu.VMEM((4, K, LANES), F32),
            pltpu.VMEM((2, AUX, LANES), F32),
            pltpu.SemaphoreType.DMA((6,)),
        ],
        compiler_params=params(),
        name="pack",
    )(in_hbm(probes.reshape(K * rows, W)), in_hbm(cls2), in_hbm(w2))
    y0, y1 = paired(y0, "gy", 0), paired(y1, "gy", 1)
    q0, q1, x0, x1 = pl.pallas_call(
        functools.partial(send_kernel, K, NZ, X),
        out_shape=(shape((q_rows, LANES), BF16),) * 2 + (shape((x_rows, W), BF16),) * 2,
        in_specs=[VMEM] * 5,
        out_specs=(VMEM,) * 4,
        scratch_shapes=[pltpu.VMEM((2 * NZ * SUB, LANES), F32)],
        compiler_params=params(),
        name="send",
    )(pt, cg, wg, y0, y1)
    q0 = paired(q0, "gx", 0)
    q1 = paired(q1, "gx", 1)
    x0 = paired(x0, "gx", 0)
    x1 = paired(x1, "gx", 1, False)
    factors = shape((per, levels * LANES, W), BF16)
    fr, fl = pl.pallas_call(
        functools.partial(prep_kernel, levels, R),
        out_shape=(factors, factors),
        in_specs=[VMEM, pl.BlockSpec(memory_space=pltpu.SMEM), VMEM, VMEM],
        out_specs=(VMEM, VMEM),
        cost_estimate=cost(1 << 20, 2 << 20),
        compiler_params=params(),
        name="prep",
    )(y0, block_ranks, prior_right, prior_left)
    slab = shape((2, rows * K, LANES), F32)
    firsts = shape((2, NZ * wide * K, LANES), F32)
    pair = shape((2, K, LANES), F32)
    coefs = shape((14, 2, *square), F32)
    s, t, cf, hp, ht, acc = pl.pallas_call(
        functools.partial(inner_kernel, K, NZ, X, R),
        out_shape=(slab, firsts, coefs, pair, pair, shape((groups, NZ * K, levels * LANES), F32)),
        in_specs=[HBM] + [VMEM] * 9,
        out_specs=(VMEM,) * 6,
        scratch_shapes=[pltpu.VMEM((4, *square), F32)] * 3
        + [
            pltpu.VMEM((3, 2, y_rows, LANES), F32),
            pltpu.VMEM((2, 2 * NZ * SUB, LANES), F32),
            pltpu.SMEM(class_table.shape, F32),
            pltpu.SemaphoreType.DMA,
        ],
        cost_estimate=cost(1 << 30, 20 << 20),
        compiler_params=params(),
        name="inner",
    )(in_hbm(class_table), pt, y0, y1, q0, q1, own, cg, wg, fr)
    side = shape((levels, groups, NZ * K, LANES), BF16)
    _, _, s, v = pl.pallas_call(
        functools.partial(edge_kernel, K, NZ, X, R),
        out_shape=(shape(pt.shape, F32), firsts, slab, side),
        in_specs=[VMEM] * 10,
        out_specs=(VMEM,) * 4,
        input_output_aliases={0: 0, 1: 1, 2: 2},
        compiler_params=params(),
        name="edge",
    )(pt, t, s, x0, x1, cf, hp, ht, acc, fr)
    share = rows // GRAM_PARTS
    parts = []

    def gram_part(i, *after):
        return pl.pallas_call(
            functools.partial(gram_kernel, K, i * share, share),
            out_shape=shape((K, LANES), F32),
            in_specs=[VMEM] * (2 + len(after)),
            out_specs=VMEM,
            cost_estimate=cost(2 * 300 * K * share * W, 8 << 20),
            compiler_params=params(),
        )(s, prior_block, *after)

    parts.append(gram_part(0))
    sibs = []
    pending = v
    for l in range(levels):
        got = exchanged(pending, "gy", 2**l)
        if l == 0:
            first_got = got
        sibs.append(got[0])
        pending = (pending[1:].astype(F32) + got[1:].astype(F32)).astype(BF16)
    parts += [gram_part(i, first_got) for i in range(1, GRAM_PARTS)]
    u = pl.pallas_call(
        functools.partial(left_kernel, K, NZ, X, R),
        out_shape=side,
        in_specs=[VMEM] * 3,
        out_specs=VMEM,
        cost_estimate=cost(1 << 28, 8 << 20),
        compiler_params=params(),
        name="left",
    )(first_got, s, fl)
    gx = pl.pallas_call(
        functools.partial(couple_kernel, K, GRAM_PARTS),
        out_shape=shape((K, LANES), F32),
        in_specs=[VMEM] * (1 + GRAM_PARTS + levels),
        out_specs=VMEM,
        compiler_params=params(),
        name="couple",
    )(u, *parts, *sibs)
    gx = summed(gx)
    basis, projected = pl.pallas_call(
        functools.partial(finish_kernel, K, NZ, X, cells),
        out_shape=(shape((K, NZ, X, W), F32), shape((K, K), F32)),
        in_specs=[VMEM] * 2,
        out_specs=(HBM, VMEM),
        scratch_shapes=[pltpu.VMEM((2, NZ, K * X, LANES), F32), pltpu.SemaphoreType.DMA((NZ, 2))],
        compiler_params=params(),
        name="finish",
    )(gx, s)
    return basis, projected


def solution(mesh):
    return jax.shard_map(
        shards,
        mesh=mesh,
        in_specs=(
            P(None, None, "gx", "gy"),
            P(None, "gx", "gy"),
            P(),
            P(None, "gx", "gy"),
            P("gy", None),
            P(None, None, "gy"),
            P(None, None, "gy"),
            P(),
        ),
        out_specs=(P(None, None, "gx", "gy"), P()),
        check_vma=False,
    )
```

```python
import functools
import jax
import jax.numpy as jnp
from jax import lax
from jax.experimental import pallas as pl
from jax.experimental.pallas import tpu as pltpu
from jax.sharding import PartitionSpec as P

HIGH = lax.Precision.HIGHEST
F32 = jnp.float32
BF16 = jnp.bfloat16
LANES = 128
SUB = 8
GROUP = 32
REACH = 3
AXES = ("gy", "gx")
UNROLL_ONE = 7
UNROLL_TWO = 3
UNROLL_GRAM = 8
NLINES = 4
GRAM_PARTS = 2
AUX = 16
VMEM = pl.BlockSpec(memory_space=pltpu.VMEM)
HBM = pl.BlockSpec(memory_space=pltpu.HBM)


def lanes_of(shape):
    return lax.broadcasted_iota(jnp.int32, shape, len(shape) - 1)


def halves(v):
    hi = v.astype(BF16)
    return hi, (v - hi.astype(F32)).astype(BF16)


def nt(a, b, precision=None):
    return lax.dot_general(a, b, (((1,), (1,)), ((), ())), precision=precision, preferred_element_type=F32)


def pack_kernel(K, NZ, X, p_hbm, cls_hbm, w_hbm, pt_ref, cg_ref, wg_ref, own_ref, y0_ref, y1_ref, p_ref, cls_ref, w_ref, edge, yaux, sem):
    rows, ext = NZ * X, X + 4
    parts = K // SUB
    step = SUB * rows
    loads = [pltpu.make_async_copy(cls_hbm, cls_ref, sem.at[parts]), pltpu.make_async_copy(w_hbm, w_ref, sem.at[parts + 1])]
    for i in range(parts):
        loads.append(pltpu.make_async_copy(p_hbm.at[pl.ds(i * step, step)], p_ref.at[pl.ds(i * step, step)], sem.at[i]))
    for load in loads:
        load.start()
    loads[0].wait()
    loads[1].wait()
    odd = lax.rem(lax.axis_index("gy"), 2)
    turned = []
    for source, grid in ((cls_ref, cg_ref), (w_ref, wg_ref)):
        for h in range(2):
            grid[h] = jnp.zeros((LANES, LANES), F32)
        for z in range(NZ):
            v = source[z * X : (z + 1) * X, :].astype(F32)
            if source is cls_ref:
                v = v + 1.0
            at = z * GROUP + REACH
            for h in range(2):
                grid[h, at : at + X, :] = v[:, h * LANES : (h + 1) * LANES]
        turned.append(jnp.where(lanes_of((LANES, LANES)) < LANES // 2, grid[0], grid[1]).T)
    yaux[...] = jnp.zeros_like(yaux)
    for side in range(2):
        at = (0, 1, 2) if side == 0 else (LANES - 1, LANES - 2, LANES - 3)
        for d in range(3):
            yaux[side, d : d + 1, :] = turned[0][at[d] : at[d] + 1, :]
        w_hi, w_lo = halves(turned[1][at[0] : at[0] + 1, :])
        yaux[side, 3:4, :] = w_hi.astype(F32)
        yaux[side, 4:5, :] = w_lo.astype(F32)
    lane = lanes_of((SUB, LANES))
    for kt in range(parts):
        loads[2 + kt].wait()
        for k in range(kt * SUB, (kt + 1) * SUB):
            v = p_ref[k * rows : (k + 1) * rows, :].astype(F32)
            for z in range(NZ):
                for h in range(2):
                    pt_ref[h, pl.ds((z * ext + 2) * K + k, X, stride=K), :] = v[z * X : (z + 1) * X, h * LANES : (h + 1) * LANES]
        out = [jnp.zeros((SUB, LANES), F32) for _ in range(4)]
        for z in range(NZ):
            for x in range(X):
                row = (z * ext + 2 + x) * K + kt * SUB
                to = z * GROUP + x + REACH
                here = lane == to
                left, right = pt_ref[0, row : row + SUB, :], pt_ref[1, row : row + SUB, :]
                for i, (tile, col) in enumerate(((left, 0), (left, 1), (right, LANES - 1), (right, LANES - 2))):
                    out[i] = jnp.where(here, pltpu.roll(tile, (to - col) % LANES, 1), out[i])
        for i in range(4):
            edge[i, kt * SUB : (kt + 1) * SUB, :] = out[i]
        own_ref[0, kt * SUB : (kt + 1) * SUB, :] = out[0]
        own_ref[1, kt * SUB : (kt + 1) * SUB, :] = out[2]
    for m, ref in enumerate((y0_ref, y1_ref)):
        side = side_of(m, odd)
        for d in range(2):
            ref[d * K : (d + 1) * K, :] = edge[2 * side + d].astype(BF16)
        ref[2 * K : 2 * K + AUX, :] = yaux[side].astype(BF16)


def side_of(m, odd):
    return 1 - odd if m == 0 else odd


def send_kernel(K, NZ, X, pt_ref, cg_ref, wg_ref, y0_ref, y1_ref, q0_ref, q1_ref, x0_ref, x1_ref, aux):
    ext = X + 4
    odd = lax.rem(lax.axis_index("gx"), 2)
    for m, ref in enumerate((q0_ref, q1_ref)):
        side = side_of(m, odd)
        for n, got in enumerate((y0_ref, y1_ref)):
            at = n * (K + AUX)
            ref[at : at + K, :] = got[:K, :]
            ref[at + K : at + K + AUX, :] = got[2 * K : 2 * K + AUX, :]
        aux[...] = jnp.zeros_like(aux)
        for h in range(2):
            for z in range(NZ):
                to = (h * NZ + z) * SUB
                for d in range(3):
                    aux[to + d : to + d + 1, :] = cg_ref[h, pl.ds(z * GROUP + REACH + side * (X - 3) + d, 1), :]
                w_hi, w_lo = halves(wg_ref[h, pl.ds(z * GROUP + REACH + side * (X - 1), 1), :])
                aux[to + 3 : to + 4, :] = w_hi.astype(F32)
                aux[to + 4 : to + 5, :] = w_lo.astype(F32)
        ref[2 * (K + AUX) :, :] = aux[...].astype(BF16)
    for m, ref in enumerate((x0_ref, x1_ref)):
        side = side_of(m, odd)
        for z in range(NZ):
            for i in range(2):
                row = pl.multiple_of((z * ext + 2 + side * (X - 2) + i) * K, SUB)
                for h in range(2):
                    ref[(z * 2 + i) * K : (z * 2 + i + 1) * K, h * LANES : (h + 1) * LANES] = pt_ref[h, pl.ds(row, K), :].astype(BF16)


def prep_kernel(levels, R, after_ref, ranks_ref, right_ref, left_ref, fr_ref, fl_ref):
    del after_ref
    rank = lax.broadcasted_iota(jnp.int32, (R, 1), 0)
    per = fr_ref.shape[0]
    fr_ref[...] = jnp.zeros_like(fr_ref)
    fl_ref[...] = jnp.zeros_like(fl_ref)
    for l in range(levels):
        scale = float(2 * LANES * 2**l) ** -0.5
        right = jnp.where(rank < ranks_ref[l], right_ref[l] * scale, 0.0).astype(BF16)
        left = left_ref[l].astype(BF16)
        for i in range(per):
            at = l * LANES + i * R
            fr_ref[i, at : at + R, :] = right
            fl_ref[i, at : at + R, :] = left


def mult(v):
    return v if isinstance(v, int) else pl.multiple_of(v, SUB)


def stencil(NZ, z, coef_row, coefs, src, centre_row, x_step, z_step, halo, kt):
    lane = lanes_of((SUB, LANES))
    is_first, is_last = lane == 0, lane == LANES - 1

    def at(row):
        return pl.ds(mult(row), SUB)

    row = centre_row + kt * SUB
    c = [src[h, at(row), :] for h in range(2)]
    up = [src[h, at(row + x_step), :] for h in range(2)]
    down = [src[h, at(row - x_step), :] for h in range(2)]
    hl = pltpu.roll(halo[0, kt * SUB : (kt + 1) * SUB, :], LANES - coef_row, 1)
    hr = pltpu.roll(halo[1, kt * SUB : (kt + 1) * SUB, :], LANES - 1 - coef_row, 1)
    fwd = [pltpu.roll(v, LANES - 1, 1) for v in c]
    bwd = [pltpu.roll(v, 1, 1) for v in c]
    nxt = [jnp.where(is_last, fwd[1], fwd[0]), jnp.where(is_last, hr, fwd[1])]
    prv = [jnp.where(is_first, hl, bwd[0]), jnp.where(is_first, bwd[0], bwd[1])]
    out = []
    for h in range(2):
        co = coefs[h]
        acc = co[0] * c[h] + co[1] * up[h] + co[2] * down[h] + co[3] * nxt[h] + co[4] * prv[h]
        if z < NZ - 1:
            acc = acc + co[5] * src[h, at(row + z_step), :]
        if z > 0:
            acc = acc + co[6] * src[h, at(row - z_step), :]
        out.append(acc)
    return out


def line_coefs(cf, first, row):
    return [[jnp.broadcast_to(cf[first + j, h, pl.ds(row, 1), :], (SUB, LANES)) for j in range(7)] for h in range(2)]


def stage_one(K, NZ, X, x, cf, pt_ref, t_ref, hp):
    ext, wide = X + 4, X + 2
    for z in range(NZ):
        coefs = line_coefs(cf, 0, z * GROUP + x + REACH)
        for kt in range(K // SUB):
            out = stencil(NZ, z, z * GROUP + x + REACH, coefs, pt_ref, (z * ext + x + 2) * K, K, ext * K, hp, kt)
            to = mult((z * wide + x + 1) * K + kt * SUB)
            for h in range(2):
                t_ref[h, pl.ds(to, SUB), :] = out[h]


def stage_two(K, NZ, X, x, cf, pt_ref, t_ref, s_ref, ht):
    ext, wide = X + 4, X + 2
    his = []
    for z in range(NZ):
        lines = []
        coefs = line_coefs(cf, 7, z * GROUP + x + REACH)
        for kt in range(K // SUB):
            out = stencil(NZ, z, z * GROUP + x + REACH, coefs, t_ref, (z * wide + x + 1) * K, K, wide * K, ht, kt)
            row = mult((z * ext + x + 2) * K + kt * SUB)
            to = mult((z * X + x) * K + kt * SUB)
            both = []
            for h in range(2):
                s = out[h] + pt_ref[h, pl.ds(row, SUB), :]
                s_ref[h, pl.ds(to, SUB), :] = s
                both.append(s)
            lines.append(jnp.concatenate(both, 1))
        his.append(jnp.concatenate(lines, 0).astype(BF16))
    return jnp.concatenate(his, 0)


def merged(own, from_left, from_right):
    X = GROUP // 2
    m = lanes_of(own.shape) % GROUP
    left = pltpu.roll(from_left, LANES - X, 1)
    right = pltpu.roll(from_right, X, 1)
    out = jnp.where(m < X + REACH, own, jnp.where(m < X + 2 * REACH, right, 0.0))
    return jnp.where(m < REACH, left, out)


def inner_kernel(
    K, NZ, X, R,
    table_hbm, pt_ref, y0_ref, y1_ref, q0_ref, q1_ref, own_ref, cin_ref, win_ref, fr_ref,
    s_ref, t_ref, cf, hp, ht, acc_ref, cg, wg, rg, ys, xs, table_ref, sem,
):
    sq = (LANES, LANES)
    lane_sq = lanes_of(sq)
    load = pltpu.make_async_copy(table_hbm, table_ref, sem)
    load.start()
    place = [lax.axis_index(axis) for axis in ("gx", "gy")]
    last = [lax.axis_size(axis) - 1 for axis in ("gx", "gy")]
    odd = [lax.rem(v, 2) for v in place]

    def there(axis, side):
        edge = lax.select(side == 0, place[axis], last[axis] - place[axis])
        return lax.select(edge > 0, jnp.float32(1.0), jnp.float32(0.0))

    for m, ref in enumerate((y0_ref, y1_ref)):
        side = side_of(m, odd[1])
        y_there = there(1, side)
        ys[0, side] = ref[...].astype(F32) * y_there
        for n, relay in enumerate((q0_ref, q1_ref)):
            x_side = side_of(n, odd[0])
            factor = y_there * there(0, x_side)
            at = m * (K + AUX)
            ys[1 + x_side, side, :K, :] = relay[at : at + K, :].astype(F32) * factor
            ys[1 + x_side, side, 2 * K :, :] = relay[at + K : at + K + AUX, :].astype(F32) * factor
    for n, relay in enumerate((q0_ref, q1_ref)):
        x_side = side_of(n, odd[0])
        xs[x_side] = relay[2 * (K + AUX) :, :].astype(F32) * there(0, x_side)
    for h in range(2):
        cg[1 + h] = cin_ref[h]
        wg[1 + h] = win_ref[h]
    for side in range(2):
        for z in range(NZ):
            for h in range(2):
                a = (h * NZ + z) * SUB
                start = z * GROUP + side * (X + REACH)
                cg[1 + h, start : start + REACH, :] = xs[side, a : a + REACH, :]
                beside = z * GROUP + REACH - 1 + side * (X + 1)
                wg[1 + h, beside : beside + 1, :] = xs[side, a + 3 : a + 4, :] + xs[side, a + 4 : a + 5, :]
    spread = jnp.zeros(sq, F32)
    row_sq = lax.broadcasted_iota(jnp.int32, sq, 0)
    spread_w = jnp.zeros(sq, F32)
    for side in range(2):
        rows = merged(*(ys[n, side, 2 * K : 2 * K + AUX, :] for n in range(3)))
        at = (LANES - 1, LANES - 2, LANES - 3) if side == 0 else (0, 1, 2)
        for d in range(3):
            spread = jnp.where(row_sq == at[d], rows[d : d + 1, :], spread)
        spread_w = jnp.where(row_sq == at[0], rows[3:4, :] + rows[4:5, :], spread_w)
    y_class, y_weight = spread.T, spread_w.T
    keep = (lane_sq >= LANES // 2, lane_sq < LANES // 2)
    for side in range(2):
        cg[3 * side] = jnp.where(keep[side], y_class, 0.0)
        wg[3 * side] = jnp.where(keep[side], y_weight, 0.0)
    load.wait()
    for t in range(4):
        ids = cg[t]
        cond = jnp.zeros(sq, F32)
        for j in range(table_ref.shape[0]):
            cond = jnp.where(ids == float(j + 1), table_ref[j], cond)
        cg[t] = cond

    zeros_g = jnp.zeros((GROUP, LANES), F32)

    def ahead(ref, t):
        nxt = ref[t + 1] if t < 3 else jnp.zeros(sq, F32)
        return jnp.where(lane_sq == LANES - 1, pltpu.roll(nxt, LANES - 1, 1), pltpu.roll(ref[t], LANES - 1, 1))

    def behind(ref, t):
        prv = ref[t - 1] if t > 0 else jnp.zeros(sq, F32)
        return jnp.where(lane_sq == 0, pltpu.roll(prv, 1, 1), pltpu.roll(ref[t], 1, 1))

    def around(ref, t):
        v = ref[t]
        return [
            pltpu.roll(v, LANES - 1, 0),
            pltpu.roll(v, 1, 0),
            ahead(ref, t),
            behind(ref, t),
            jnp.concatenate([v[GROUP:], zeros_g], 0),
            jnp.concatenate([zeros_g, v[:-GROUP]], 0),
        ]

    for t in range(4):
        c = cg[t]
        total = jnp.ones(sq, F32)
        for other in around(cg, t):
            total = total + 0.5 * (c + other)
        rg[t] = 1.0 / total
    picked = jnp.zeros(sq, F32)
    for t in range(4):
        c, r, w = cg[t], rg[t], wg[t]
        pairs = zip(around(cg, t), around(rg, t))
        terms = [r] + [0.5 * (c + c_n) * (r * r_n) for c_n, r_n in pairs]
        for j, term in enumerate(terms):
            if t in (1, 2):
                cf[j, t - 1] = w * term
                cf[7 + j, t - 1] = term
            else:
                to = j if t == 0 else 8 + j
                start = LANES - 1 if t == 0 else 0
                picked = jnp.where(lane_sq == to, pltpu.roll(w * term, (to - start) % LANES, 1), picked)
    edge_cf = picked.T
    for side in range(2):
        p1 = merged(*(ys[n, side, :K, :] for n in range(3)))
        p2 = ys[0, side, K : 2 * K, :]
        p0 = own_ref[side]
        y_next, y_prev = (p0, p2) if side == 0 else (p2, p0)
        parts = [
            p1,
            pltpu.roll(p1, LANES - 1, 1),
            pltpu.roll(p1, 1, 1),
            y_next,
            y_prev,
            pltpu.roll(p1, LANES - GROUP, 1),
            pltpu.roll(p1, GROUP, 1),
        ]
        total = edge_cf[8 * side : 8 * side + 1, :] * parts[0]
        for j in range(1, 7):
            total = total + edge_cf[8 * side + j : 8 * side + j + 1, :] * parts[j]
        hp[side] = p1
        ht[side] = total


    def first_lines(i, carry):
        stage_one(K, NZ, X, i, cf, pt_ref, t_ref, hp)
        return carry

    lax.fori_loop(1, X - 1, first_lines, 0, unroll=UNROLL_ONE)
    acc_ref[...] = jnp.zeros_like(acc_ref)
    per = LANES // R // 2

    def second_lines(i, carry):
        for half in range(2):
            lines = stage_two(K, NZ, X, 2 * i + half, cf, pt_ref, t_ref, s_ref, ht)
            group = lax.div(i, per)
            acc_ref[group] = acc_ref[group] + nt(lines, fr_ref[2 * lax.rem(i, per) + half])
        return carry

    lax.fori_loop(1, X // 2 - 1, second_lines, 0, unroll=UNROLL_TWO)


def edge_kernel(K, NZ, X, R, pt_in, t_in, s_in, x0_ref, x1_ref, cf, hp, ht, acc_ref, fr_ref, pt_ref, t_ref, s_ref, v_ref):
    ext = X + 4
    odd = lax.rem(lax.axis_index("gx"), 2)
    for m, ref in enumerate((x0_ref, x1_ref)):
        side = side_of(m, odd)
        for z in range(NZ):
            for i in range(2):
                at = pl.multiple_of((z * ext + i + side * (X + 2)) * K, SUB)
                for h in range(2):
                    cut = (slice((z * 2 + i) * K, (z * 2 + i + 1) * K), slice(h * LANES, (h + 1) * LANES))
                    pt_ref[h, pl.ds(at, K), :] = ref[cut].astype(F32)
    for x in (-1, 0, X - 1, X):
        stage_one(K, NZ, X, x, cf, pt_ref, t_ref, hp)
    per = LANES // R
    sums = [acc_ref[g] for g in range(X // per)]
    for x in (0, 1, X - 2, X - 1):
        lines = stage_two(K, NZ, X, x, cf, pt_ref, t_ref, s_ref, ht)
        sums[x // per] = sums[x // per] + nt(lines, fr_ref[x % per])
    for g, total in enumerate(sums):
        for l in range(v_ref.shape[0]):
            v_ref[l, g] = total[:, l * LANES : (l + 1) * LANES].astype(BF16)


def left_kernel(K, NZ, X, R, after_ref, s_ref, fl_ref, u_ref):
    del after_ref
    per = LANES // R
    for g in range(X // per):
        total = None
        for i in range(per):
            x = g * per + i
            lines = []
            for z in range(NZ):
                at = (z * X + x) * K
                lines.append(jnp.concatenate([s_ref[h, at : at + K, :] for h in range(2)], 1).astype(BF16))
            term = nt(jnp.concatenate(lines, 0), fl_ref[i])
            total = term if total is None else total + term
        for l in range(u_ref.shape[0]):
            u_ref[l, g] = total[:, l * LANES : (l + 1) * LANES].astype(BF16)


def gram_kernel(K, first, count, s_ref, block_ref, *refs):
    gx_ref = refs[-1]
    leaf_matrix = block_ref[...].astype(BF16)

    def chunk(i, carry):
        gram, mixed = carry
        his = []
        for n in range(NLINES):
            at = pl.multiple_of((first + i * NLINES + n) * K, SUB)
            hi, lo = halves(jnp.concatenate([s_ref[h, pl.ds(at, K), :] for h in range(2)], 1))
            gram = gram + nt(hi, jnp.concatenate([hi, lo], 0))
            his.append(hi)
        leaf = nt(jnp.concatenate(his, 0), leaf_matrix).astype(BF16)
        for n in range(NLINES):
            mixed = mixed + nt(his[n], leaf[n * K : (n + 1) * K])
        return gram, mixed

    init = (jnp.zeros((K, 2 * K), F32), jnp.zeros((K, K), F32))
    gram, mixed = lax.fori_loop(0, count // NLINES, chunk, init, unroll=UNROLL_GRAM)
    low = gram[:, K:]
    gx_ref[...] = jnp.zeros_like(gx_ref)
    gx_ref[:, :K] = gram[:, :K] + low + low.T
    gx_ref[:, LANES // 2 : LANES // 2 + K] = mixed


def couple_kernel(K, parts, u_ref, *refs):
    gx_refs, sib_refs, out_ref = refs[:parts], refs[parts:-1], refs[-1]
    total = jnp.zeros((K, K), F32)
    for l, ref in enumerate(sib_refs):
        for g in range(u_ref.shape[1]):
            for at in range(0, u_ref.shape[2], K):
                total = total + nt(u_ref[l, g, at : at + K, :], ref[g, at : at + K, :])
    out_ref[...] = sum(ref[...] for ref in gx_refs)
    at = LANES // 2
    out_ref[:, at : at + K] = out_ref[:, at : at + K] + total


def eliminated(K, aug):
    tile = (SUB, LANES)
    tiles = [aug[i : i + SUB] for i in range(0, K, SUB)]
    sub = lax.broadcasted_iota(jnp.int32, tile, 0)
    for first in range(K // SUB):
        rest = range(first, K // SUB)
        j = first * SUB
        columns = [[jnp.broadcast_to(tiles[i][:, j + q : j + q + 1], tile) for i in rest] for q in range(SUB)]
        rows = [jnp.broadcast_to(tiles[first][q : q + 1, :], tile) for q in range(SUB)]
        block = [[jnp.broadcast_to(columns[t][0][q : q + 1, :], tile) for t in range(SUB)] for q in range(SUB)]
        for q in range(SUB):
            inverse = 1.0 / block[q][q]
            multiples = [c * inverse for c in columns[q]]
            for t in range(q + 1, SUB):
                factor = block[q][t] * inverse
                for u in range(t, SUB):
                    block[t][u] = block[t][u] - factor * block[q][u]
                rows[t] = rows[t] - factor * rows[q]
                columns[t] = [c - m * block[q][t] for c, m in zip(columns[t], multiples)]
            columns[q] = multiples
        for n, i in enumerate(rest):
            for q in range(SUB):
                m = columns[q][n]
                if n == 0:
                    if q == SUB - 1:
                        continue
                    m = jnp.where(sub > q, m, 0.0)
                tiles[i] = tiles[i] - m * rows[q]
    return jnp.concatenate(tiles, 0)


def finish_kernel(K, NZ, X, cells, gx_ref, s_ref, basis_ref, proj_ref, out, sem):
    lane = lanes_of((K, LANES))
    row = lax.broadcasted_iota(jnp.int32, (K, LANES), 0)
    half = LANES // 2
    gx = gx_ref[...] * (1.0 / cells)
    gram = gx[:, :K]
    mixed = gram + gx[:, half : half + K]
    aug = jnp.where(lane < K, gx, jnp.where(lane - half == row, 1.0, 0.0))
    aug = eliminated(K, aug)
    pivots = jnp.sum(jnp.where(lane == row, aug, 0.0), axis=1, keepdims=True)
    inverse = aug[:, half : half + K] * lax.rsqrt(pivots)
    left = jnp.dot(inverse, mixed, precision=HIGH, preferred_element_type=F32)
    proj_ref[...] = nt(left, inverse, precision=HIGH)
    i_hi, i_lo = halves(inverse)
    lhs = jnp.concatenate([i_hi, i_lo, i_hi], 1)
    copies = []
    for z in range(NZ):

        def line(x, carry, z=z):
            at = pl.multiple_of((z * X + x) * K, SUB)
            s = jnp.concatenate([s_ref[h, pl.ds(at, K), :] for h in range(2)], 1)
            hi, lo = halves(s)
            b = jnp.dot(lhs, jnp.concatenate([hi, hi, lo], 0), preferred_element_type=F32)
            for h in range(2):
                out[h, z, pl.ds(x, K, stride=X), :] = b[:, h * LANES : (h + 1) * LANES]
            return carry

        lax.fori_loop(0, X, line, 0, unroll=True)
        for h in range(2):
            for _ in range(1):
                copies.append(
                    pltpu.make_async_copy(
                        out.at[h, z].reshape(K, X, LANES), basis_ref.at[:, z, :, pl.ds(h * LANES, LANES)], sem.at[z, h]
                    )
                )
                copies[-1].start()
    for c in copies:
        c.wait()


def in_hbm(v):
    return pltpu.with_memory_space_constraint(v, pltpu.HBM)


def exchanged(v, axis, bits):
    return lax.ppermute(v, axis, [(i, i ^ bits) for i in range(lax.axis_size(axis))])


def paired(v, axis, first, ring=True):
    n = lax.axis_size(axis)
    swaps = [(i, i + 1) for i in range(first, n - 1, 2)]
    if first and ring:
        swaps = swaps + [(0, n - 1)]
    return lax.ppermute(v, axis, swaps + [(j, i) for i, j in swaps])


def summed(v):
    for axis in AXES:
        bit = 1
        while bit < lax.axis_size(axis):
            v = v + exchanged(v, axis, bit)
            bit *= 2
    return v


def shards(probes, classes, class_table, weights, prior_block, prior_left, prior_right, block_ranks):
    K, NZ, X, W = probes.shape
    R = prior_left.shape[1]
    levels = lax.axis_size("gy").bit_length() - 1
    cells = float(NZ * X * W * lax.axis_size("gx") * lax.axis_size("gy"))
    rows, ext, wide = NZ * X, X + 4, X + 2
    shape = jax.ShapeDtypeStruct
    cls2, w2 = classes.reshape(rows, W), weights.reshape(rows, W)
    params = functools.partial(pltpu.CompilerParams, vmem_limit_bytes=32 << 20)
    y_rows, x_rows = 2 * K + AUX, 2 * NZ * K
    q_rows = 2 * (K + AUX) + 2 * NZ * SUB
    square = (LANES, LANES)
    per = LANES // R
    groups = X // per

    def cost(flops, nbytes=4 << 20):
        return pl.CostEstimate(flops=flops, bytes_accessed=nbytes, transcendentals=0)

    pt, cg, wg, own, y0, y1 = pl.pallas_call(
        functools.partial(pack_kernel, K, NZ, X),
        out_shape=(
            shape((2, NZ * ext * K, LANES), F32),
            shape((2, *square), F32),
            shape((2, *square), F32),
            shape((2, K, LANES), F32),
            shape((y_rows, LANES), BF16),
            shape((y_rows, LANES), BF16),
        ),
        in_specs=[HBM] * 3,
        out_specs=(VMEM,) * 6,
        scratch_shapes=[
            pltpu.VMEM((K * rows, W), BF16),
            pltpu.VMEM((rows, W), jnp.int32),
            pltpu.VMEM((rows, W), F32),
            pltpu.VMEM((4, K, LANES), F32),
            pltpu.VMEM((2, AUX, LANES), F32),
            pltpu.SemaphoreType.DMA((K // SUB + 2,)),
        ],
        compiler_params=params(),
        name="pack",
    )(in_hbm(probes.reshape(K * rows, W)), in_hbm(cls2), in_hbm(w2))
    y0, y1 = paired(y0, "gy", 0), paired(y1, "gy", 1)
    q0, q1, x0, x1 = pl.pallas_call(
        functools.partial(send_kernel, K, NZ, X),
        out_shape=(shape((q_rows, LANES), BF16),) * 2 + (shape((x_rows, W), BF16),) * 2,
        in_specs=[VMEM] * 5,
        out_specs=(VMEM,) * 4,
        scratch_shapes=[pltpu.VMEM((2 * NZ * SUB, LANES), F32)],
        compiler_params=params(),
        name="send",
    )(pt, cg, wg, y0, y1)
    q0 = paired(q0, "gx", 0)
    q1 = paired(q1, "gx", 1)
    x0 = paired(x0, "gx", 0)
    x1 = paired(x1, "gx", 1, False)
    factors = shape((per, levels * LANES, W), BF16)
    fr, fl = pl.pallas_call(
        functools.partial(prep_kernel, levels, R),
        out_shape=(factors, factors),
        in_specs=[VMEM, pl.BlockSpec(memory_space=pltpu.SMEM), VMEM, VMEM],
        out_specs=(VMEM, VMEM),
        cost_estimate=cost(1 << 20, 2 << 20),
        compiler_params=params(),
        name="prep",
    )(y0, block_ranks, prior_right, prior_left)
    slab = shape((2, rows * K, LANES), F32)
    firsts = shape((2, NZ * wide * K, LANES), F32)
    pair = shape((2, K, LANES), F32)
    coefs = shape((14, 2, *square), F32)
    s, t, cf, hp, ht, acc = pl.pallas_call(
        functools.partial(inner_kernel, K, NZ, X, R),
        out_shape=(slab, firsts, coefs, pair, pair, shape((groups, NZ * K, levels * LANES), F32)),
        in_specs=[HBM] + [VMEM] * 9,
        out_specs=(VMEM,) * 6,
        scratch_shapes=[pltpu.VMEM((4, *square), F32)] * 3
        + [
            pltpu.VMEM((3, 2, y_rows, LANES), F32),
            pltpu.VMEM((2, 2 * NZ * SUB, LANES), F32),
            pltpu.SMEM(class_table.shape, F32),
            pltpu.SemaphoreType.DMA,
        ],
        cost_estimate=cost(1 << 30, 20 << 20),
        compiler_params=params(),
        name="inner",
    )(in_hbm(class_table), pt, y0, y1, q0, q1, own, cg, wg, fr)
    side = shape((levels, groups, NZ * K, LANES), BF16)
    _, _, s, v = pl.pallas_call(
        functools.partial(edge_kernel, K, NZ, X, R),
        out_shape=(shape(pt.shape, F32), firsts, slab, side),
        in_specs=[VMEM] * 10,
        out_specs=(VMEM,) * 4,
        input_output_aliases={0: 0, 1: 1, 2: 2},
        compiler_params=params(),
        name="edge",
    )(pt, t, s, x0, x1, cf, hp, ht, acc, fr)
    share = rows // GRAM_PARTS
    parts = []

    def gram_part(i, *after):
        return pl.pallas_call(
            functools.partial(gram_kernel, K, i * share, share),
            out_shape=shape((K, LANES), F32),
            in_specs=[VMEM] * (2 + len(after)),
            out_specs=VMEM,
            cost_estimate=cost(2 * 300 * K * share * W, 8 << 20),
            compiler_params=params(),
        )(s, prior_block, *after)

    parts.append(gram_part(0))
    sibs = []
    pending = v
    for l in range(levels):
        got = exchanged(pending, "gy", 2**l)
        if l == 0:
            first_got = got
        sibs.append(got[0])
        pending = (pending[1:].astype(F32) + got[1:].astype(F32)).astype(BF16)
    parts += [gram_part(i, first_got) for i in range(1, GRAM_PARTS)]
    u = pl.pallas_call(
        functools.partial(left_kernel, K, NZ, X, R),
        out_shape=side,
        in_specs=[VMEM] * 3,
        out_specs=VMEM,
        cost_estimate=cost(1 << 28, 8 << 20),
        compiler_params=params(),
        name="left",
    )(first_got, s, fl)
    gx = pl.pallas_call(
        functools.partial(couple_kernel, K, GRAM_PARTS),
        out_shape=shape((K, LANES), F32),
        in_specs=[VMEM] * (1 + GRAM_PARTS + levels),
        out_specs=VMEM,
        compiler_params=params(),
        name="couple",
    )(u, *parts, *sibs)
    gx = summed(gx)
    basis, projected = pl.pallas_call(
        functools.partial(finish_kernel, K, NZ, X, cells),
        out_shape=(shape((K, NZ, X, W), F32), shape((K, K), F32)),
        in_specs=[VMEM] * 2,
        out_specs=(HBM, VMEM),
        scratch_shapes=[pltpu.VMEM((2, NZ, K * X, LANES), F32), pltpu.SemaphoreType.DMA((NZ, 2))],
        compiler_params=params(),
        name="finish",
    )(gx, s)
    return basis, projected


def solution(mesh):
    return jax.shard_map(
        shards,
        mesh=mesh,
        in_specs=(
            P(None, None, "gx", "gy"),
            P(None, "gx", "gy"),
            P(),
            P(None, "gx", "gy"),
            P("gy", None),
            P(None, None, "gy"),
            P(None, None, "gy"),
            P(),
        ),
        out_specs=(P(None, None, "gx", "gy"), P()),
        check_vma=False,
    )
```

```python
import functools
import jax
import jax.numpy as jnp
from jax import lax
from jax.experimental import pallas as pl
from jax.experimental.pallas import tpu as pltpu
from jax.sharding import PartitionSpec as P

HIGH = lax.Precision.HIGHEST
F32 = jnp.float32
BF16 = jnp.bfloat16
LANES = 128
SUB = 8
GROUP = 32
REACH = 3
UNROLL_ONE = 14
UNROLL_TWO = 3
UNROLL_GRAM = 8
NLINES = 4
GRAM_PARTS = 2
AUX = 16
VMEM = pl.BlockSpec(memory_space=pltpu.VMEM)
HBM = pl.BlockSpec(memory_space=pltpu.HBM)


def lanes_of(shape):
    return lax.broadcasted_iota(jnp.int32, shape, len(shape) - 1)


def halves(v):
    hi = v.astype(BF16)
    return hi, (v - hi.astype(F32)).astype(BF16)


def nt(a, b, precision=None):
    return lax.dot_general(a, b, (((1,), (1,)), ((), ())), precision=precision, preferred_element_type=F32)


def pack_kernel(K, NZ, X, p_hbm, cls_hbm, w_hbm, pt_ref, cg_ref, wg_ref, own_ref, y0_ref, y1_ref, p_ref, cls_ref, w_ref, edge, yaux, sem):
    rows, ext = NZ * X, X + 4
    parts = K // SUB
    step = SUB * rows
    loads = [pltpu.make_async_copy(cls_hbm, cls_ref, sem.at[parts]), pltpu.make_async_copy(w_hbm, w_ref, sem.at[parts + 1])]
    for i in range(parts):
        loads.append(pltpu.make_async_copy(p_hbm.at[pl.ds(i * step, step)], p_ref.at[pl.ds(i * step, step)], sem.at[i]))
    for load in loads:
        load.start()
    loads[0].wait()
    loads[1].wait()
    odd = lax.rem(lax.axis_index("gy"), 2)
    turned = []
    for source, grid in ((cls_ref, cg_ref), (w_ref, wg_ref)):
        for h in range(2):
            grid[h] = jnp.zeros((LANES, LANES), F32)
        for z in range(NZ):
            v = source[z * X : (z + 1) * X, :].astype(F32)
            if source is cls_ref:
                v = v + 1.0
            at = z * GROUP + REACH
            for h in range(2):
                grid[h, at : at + X, :] = v[:, h * LANES : (h + 1) * LANES]
        turned.append(jnp.where(lanes_of((LANES, LANES)) < LANES // 2, grid[0], grid[1]).T)
    yaux[...] = jnp.zeros_like(yaux)
    for side in range(2):
        at = (0, 1, 2) if side == 0 else (LANES - 1, LANES - 2, LANES - 3)
        for d in range(3):
            yaux[side, d : d + 1, :] = turned[0][at[d] : at[d] + 1, :]
        w_hi, w_lo = halves(turned[1][at[0] : at[0] + 1, :])
        yaux[side, 3:4, :] = w_hi.astype(F32)
        yaux[side, 4:5, :] = w_lo.astype(F32)
    lane = lanes_of((SUB, LANES))
    for kt in range(parts):
        loads[2 + kt].wait()
        for k in range(kt * SUB, (kt + 1) * SUB):
            v = p_ref[k * rows : (k + 1) * rows, :].astype(F32)
            for z in range(NZ):
                for h in range(2):
                    pt_ref[h, pl.ds((z * ext + 2) * K + k, X, stride=K), :] = v[z * X : (z + 1) * X, h * LANES : (h + 1) * LANES]
        out = [jnp.zeros((SUB, LANES), F32) for _ in range(4)]
        for z in range(NZ):
            for x in range(X):
                row = (z * ext + 2 + x) * K + kt * SUB
                to = z * GROUP + x + REACH
                here = lane == to
                left, right = pt_ref[0, row : row + SUB, :], pt_ref[1, row : row + SUB, :]
                for i, (tile, col) in enumerate(((left, 0), (left, 1), (right, LANES - 1), (right, LANES - 2))):
                    out[i] = jnp.where(here, pltpu.roll(tile, (to - col) % LANES, 1), out[i])
        for i in range(4):
            edge[i, kt * SUB : (kt + 1) * SUB, :] = out[i]
        own_ref[0, kt * SUB : (kt + 1) * SUB, :] = out[0]
        own_ref[1, kt * SUB : (kt + 1) * SUB, :] = out[2]
    for m, ref in enumerate((y0_ref, y1_ref)):
        side = side_of(m, odd)
        for d in range(2):
            ref[d * K : (d + 1) * K, :] = edge[2 * side + d].astype(BF16)
        ref[2 * K : 2 * K + AUX, :] = yaux[side].astype(BF16)


def side_of(m, odd):
    return 1 - odd if m == 0 else odd


def send_kernel(K, NZ, X, pt_ref, cg_ref, wg_ref, y0_ref, y1_ref, q0_ref, q1_ref, x0_ref, x1_ref, aux):
    ext = X + 4
    odd = lax.rem(lax.axis_index("gx"), 2)
    for m, ref in enumerate((q0_ref, q1_ref)):
        side = side_of(m, odd)
        for n, got in enumerate((y0_ref, y1_ref)):
            at = n * (K + AUX)
            ref[at : at + K, :] = got[:K, :]
            ref[at + K : at + K + AUX, :] = got[2 * K : 2 * K + AUX, :]
        aux[...] = jnp.zeros_like(aux)
        for h in range(2):
            for z in range(NZ):
                to = (h * NZ + z) * SUB
                for d in range(3):
                    aux[to + d : to + d + 1, :] = cg_ref[h, pl.ds(z * GROUP + REACH + side * (X - 3) + d, 1), :]
                w_hi, w_lo = halves(wg_ref[h, pl.ds(z * GROUP + REACH + side * (X - 1), 1), :])
                aux[to + 3 : to + 4, :] = w_hi.astype(F32)
                aux[to + 4 : to + 5, :] = w_lo.astype(F32)
        ref[2 * (K + AUX) :, :] = aux[...].astype(BF16)
    for m, ref in enumerate((x0_ref, x1_ref)):
        side = side_of(m, odd)
        for z in range(NZ):
            for i in range(2):
                row = pl.multiple_of((z * ext + 2 + side * (X - 2) + i) * K, SUB)
                for h in range(2):
                    ref[(z * 2 + i) * K : (z * 2 + i + 1) * K, h * LANES : (h + 1) * LANES] = pt_ref[h, pl.ds(row, K), :].astype(BF16)


def prep_kernel(levels, R, after_ref, ranks_ref, right_ref, left_ref, fr_ref, fl_ref):
    del after_ref
    rank = lax.broadcasted_iota(jnp.int32, (R, 1), 0)
    per = fr_ref.shape[0]
    fr_ref[...] = jnp.zeros_like(fr_ref)
    fl_ref[...] = jnp.zeros_like(fl_ref)
    for l in range(levels):
        scale = float(2 * LANES * 2**l) ** -0.5
        right = jnp.where(rank < ranks_ref[l], right_ref[l] * scale, 0.0).astype(BF16)
        left = left_ref[l].astype(BF16)
        for i in range(per):
            at = l * LANES + i * R
            fr_ref[i, at : at + R, :] = right
            fl_ref[i, at : at + R, :] = left


def mult(v):
    return v if isinstance(v, int) else pl.multiple_of(v, SUB)


def stencil(NZ, z, coef_row, coefs, src, centre_row, x_step, z_step, halo, kt):
    lane = lanes_of((SUB, LANES))
    is_first, is_last = lane == 0, lane == LANES - 1

    def at(row):
        return pl.ds(mult(row), SUB)

    row = centre_row + kt * SUB
    c = [src[h, at(row), :] for h in range(2)]
    up = [src[h, at(row + x_step), :] for h in range(2)]
    down = [src[h, at(row - x_step), :] for h in range(2)]
    hl = pltpu.roll(halo[0, kt * SUB : (kt + 1) * SUB, :], LANES - coef_row, 1)
    hr = pltpu.roll(halo[1, kt * SUB : (kt + 1) * SUB, :], LANES - 1 - coef_row, 1)
    fwd = [pltpu.roll(v, LANES - 1, 1) for v in c]
    bwd = [pltpu.roll(v, 1, 1) for v in c]
    nxt = [jnp.where(is_last, fwd[1], fwd[0]), jnp.where(is_last, hr, fwd[1])]
    prv = [jnp.where(is_first, hl, bwd[0]), jnp.where(is_first, bwd[0], bwd[1])]
    out = []
    for h in range(2):
        co = coefs[h]
        acc = co[0] * c[h] + co[1] * up[h] + co[2] * down[h] + co[3] * nxt[h] + co[4] * prv[h]
        if z < NZ - 1:
            acc = acc + co[5] * src[h, at(row + z_step), :]
        if z > 0:
            acc = acc + co[6] * src[h, at(row - z_step), :]
        out.append(acc)
    return out


def line_coefs(cf, first, row):
    return [[jnp.broadcast_to(cf[first + j, h, pl.ds(row, 1), :], (SUB, LANES)) for j in range(7)] for h in range(2)]


def stage_one(K, NZ, X, x, cf, pt_ref, t_ref, hp):
    ext, wide = X + 4, X + 2
    for z in range(NZ):
        coefs = line_coefs(cf, 0, z * GROUP + x + REACH)
        for kt in range(K // SUB):
            out = stencil(NZ, z, z * GROUP + x + REACH, coefs, pt_ref, (z * ext + x + 2) * K, K, ext * K, hp, kt)
            to = mult((z * wide + x + 1) * K + kt * SUB)
            for h in range(2):
                t_ref[h, pl.ds(to, SUB), :] = out[h]


def stage_two(K, NZ, X, x, cf, pt_ref, t_ref, s_ref, ht):
    ext, wide = X + 4, X + 2
    his = []
    for z in range(NZ):
        lines = []
        coefs = line_coefs(cf, 7, z * GROUP + x + REACH)
        for kt in range(K // SUB):
            out = stencil(NZ, z, z * GROUP + x + REACH, coefs, t_ref, (z * wide + x + 1) * K, K, wide * K, ht, kt)
            row = mult((z * ext + x + 2) * K + kt * SUB)
            to = mult((z * X + x) * K + kt * SUB)
            both = []
            for h in range(2):
                s = out[h] + pt_ref[h, pl.ds(row, SUB), :]
                s_ref[h, pl.ds(to, SUB), :] = s
                both.append(s)
            lines.append(jnp.concatenate(both, 1))
        his.append(jnp.concatenate(lines, 0).astype(BF16))
    return jnp.concatenate(his, 0)


def merged(own, from_left, from_right):
    X = GROUP // 2
    m = lanes_of(own.shape) % GROUP
    left = pltpu.roll(from_left, LANES - X, 1)
    right = pltpu.roll(from_right, X, 1)
    out = jnp.where(m < X + REACH, own, jnp.where(m < X + 2 * REACH, right, 0.0))
    return jnp.where(m < REACH, left, out)


def inner_kernel(
    K, NZ, X, R,
    table_hbm, pt_ref, y0_ref, y1_ref, q0_ref, q1_ref, own_ref, cin_ref, win_ref, fr_ref,
    s_ref, t_ref, cf, hp, ht, acc_ref, cg, wg, rg, ys, xs, table_ref, sem,
):
    sq = (LANES, LANES)
    lane_sq = lanes_of(sq)
    load = pltpu.make_async_copy(table_hbm, table_ref, sem)
    load.start()
    place = [lax.axis_index(axis) for axis in ("gx", "gy")]
    last = [lax.axis_size(axis) - 1 for axis in ("gx", "gy")]
    odd = [lax.rem(v, 2) for v in place]

    def there(axis, side):
        edge = lax.select(side == 0, place[axis], last[axis] - place[axis])
        return lax.select(edge > 0, jnp.float32(1.0), jnp.float32(0.0))

    for m, ref in enumerate((y0_ref, y1_ref)):
        side = side_of(m, odd[1])
        y_there = there(1, side)
        ys[0, side] = ref[...].astype(F32) * y_there
        for n, relay in enumerate((q0_ref, q1_ref)):
            x_side = side_of(n, odd[0])
            factor = y_there * there(0, x_side)
            at = m * (K + AUX)
            ys[1 + x_side, side, :K, :] = relay[at : at + K, :].astype(F32) * factor
            ys[1 + x_side, side, 2 * K :, :] = relay[at + K : at + K + AUX, :].astype(F32) * factor
    for n, relay in enumerate((q0_ref, q1_ref)):
        x_side = side_of(n, odd[0])
        xs[x_side] = relay[2 * (K + AUX) :, :].astype(F32) * there(0, x_side)
    for h in range(2):
        cg[1 + h] = cin_ref[h]
        wg[1 + h] = win_ref[h]
    for side in range(2):
        for z in range(NZ):
            for h in range(2):
                a = (h * NZ + z) * SUB
                start = z * GROUP + side * (X + REACH)
                cg[1 + h, start : start + REACH, :] = xs[side, a : a + REACH, :]
                beside = z * GROUP + REACH - 1 + side * (X + 1)
                wg[1 + h, beside : beside + 1, :] = xs[side, a + 3 : a + 4, :] + xs[side, a + 4 : a + 5, :]
    spread = jnp.zeros(sq, F32)
    row_sq = lax.broadcasted_iota(jnp.int32, sq, 0)
    spread_w = jnp.zeros(sq, F32)
    for side in range(2):
        rows = merged(*(ys[n, side, 2 * K : 2 * K + AUX, :] for n in range(3)))
        at = (LANES - 1, LANES - 2, LANES - 3) if side == 0 else (0, 1, 2)
        for d in range(3):
            spread = jnp.where(row_sq == at[d], rows[d : d + 1, :], spread)
        spread_w = jnp.where(row_sq == at[0], rows[3:4, :] + rows[4:5, :], spread_w)
    y_class, y_weight = spread.T, spread_w.T
    keep = (lane_sq >= LANES // 2, lane_sq < LANES // 2)
    for side in range(2):
        cg[3 * side] = jnp.where(keep[side], y_class, 0.0)
        wg[3 * side] = jnp.where(keep[side], y_weight, 0.0)
    load.wait()
    for t in range(4):
        ids = cg[t]
        cond = jnp.zeros(sq, F32)
        for j in range(table_ref.shape[0]):
            cond = jnp.where(ids == float(j + 1), table_ref[j], cond)
        cg[t] = cond

    zeros_g = jnp.zeros((GROUP, LANES), F32)

    def ahead(ref, t):
        nxt = ref[t + 1] if t < 3 else jnp.zeros(sq, F32)
        return jnp.where(lane_sq == LANES - 1, pltpu.roll(nxt, LANES - 1, 1), pltpu.roll(ref[t], LANES - 1, 1))

    def behind(ref, t):
        prv = ref[t - 1] if t > 0 else jnp.zeros(sq, F32)
        return jnp.where(lane_sq == 0, pltpu.roll(prv, 1, 1), pltpu.roll(ref[t], 1, 1))

    def around(ref, t):
        v = ref[t]
        return [
            pltpu.roll(v, LANES - 1, 0),
            pltpu.roll(v, 1, 0),
            ahead(ref, t),
            behind(ref, t),
            jnp.concatenate([v[GROUP:], zeros_g], 0),
            jnp.concatenate([zeros_g, v[:-GROUP]], 0),
        ]

    for t in range(4):
        c = cg[t]
        total = jnp.ones(sq, F32)
        for other in around(cg, t):
            total = total + 0.5 * (c + other)
        rg[t] = 1.0 / total
    picked = jnp.zeros(sq, F32)
    for t in range(4):
        c, r, w = cg[t], rg[t], wg[t]
        pairs = zip(around(cg, t), around(rg, t))
        terms = [r] + [0.5 * (c + c_n) * (r * r_n) for c_n, r_n in pairs]
        for j, term in enumerate(terms):
            if t in (1, 2):
                cf[j, t - 1] = w * term
                cf[7 + j, t - 1] = term
            else:
                to = j if t == 0 else 8 + j
                start = LANES - 1 if t == 0 else 0
                picked = jnp.where(lane_sq == to, pltpu.roll(w * term, (to - start) % LANES, 1), picked)
    edge_cf = picked.T
    for side in range(2):
        p1 = merged(*(ys[n, side, :K, :] for n in range(3)))
        p2 = ys[0, side, K : 2 * K, :]
        p0 = own_ref[side]
        y_next, y_prev = (p0, p2) if side == 0 else (p2, p0)
        parts = [
            p1,
            pltpu.roll(p1, LANES - 1, 1),
            pltpu.roll(p1, 1, 1),
            y_next,
            y_prev,
            pltpu.roll(p1, LANES - GROUP, 1),
            pltpu.roll(p1, GROUP, 1),
        ]
        total = edge_cf[8 * side : 8 * side + 1, :] * parts[0]
        for j in range(1, 7):
            total = total + edge_cf[8 * side + j : 8 * side + j + 1, :] * parts[j]
        hp[side] = p1
        ht[side] = total


    def first_lines(i, carry):
        stage_one(K, NZ, X, i, cf, pt_ref, t_ref, hp)
        return carry

    lax.fori_loop(1, X - 1, first_lines, 0, unroll=UNROLL_ONE)
    acc_ref[...] = jnp.zeros_like(acc_ref)
    per = LANES // R // 2

    def second_lines(i, carry):
        for half in range(2):
            lines = stage_two(K, NZ, X, 2 * i + half, cf, pt_ref, t_ref, s_ref, ht)
            group = lax.div(i, per)
            acc_ref[group] = acc_ref[group] + nt(lines, fr_ref[2 * lax.rem(i, per) + half])
        return carry

    lax.fori_loop(1, X // 2 - 1, second_lines, 0, unroll=UNROLL_TWO)


def edge_kernel(K, NZ, X, R, pt_in, t_in, s_in, x0_ref, x1_ref, cf, hp, ht, acc_ref, fr_ref, pt_ref, t_ref, s_ref, v_ref):
    ext = X + 4
    odd = lax.rem(lax.axis_index("gx"), 2)
    for m, ref in enumerate((x0_ref, x1_ref)):
        side = side_of(m, odd)
        for z in range(NZ):
            for i in range(2):
                at = pl.multiple_of((z * ext + i + side * (X + 2)) * K, SUB)
                for h in range(2):
                    cut = (slice((z * 2 + i) * K, (z * 2 + i + 1) * K), slice(h * LANES, (h + 1) * LANES))
                    pt_ref[h, pl.ds(at, K), :] = ref[cut].astype(F32)
    for x in (-1, 0, X - 1, X):
        stage_one(K, NZ, X, x, cf, pt_ref, t_ref, hp)
    per = LANES // R
    sums = [acc_ref[g] for g in range(X // per)]
    for x in (0, 1, X - 2, X - 1):
        lines = stage_two(K, NZ, X, x, cf, pt_ref, t_ref, s_ref, ht)
        sums[x // per] = sums[x // per] + nt(lines, fr_ref[x % per])
    for g, total in enumerate(sums):
        for l in range(v_ref.shape[0]):
            v_ref[l, g] = total[:, l * LANES : (l + 1) * LANES].astype(BF16)


def left_kernel(K, NZ, X, R, after_ref, s_ref, fl_ref, u_ref):
    del after_ref
    per = LANES // R
    for g in range(X // per):
        total = None
        for i in range(per):
            x = g * per + i
            lines = []
            for z in range(NZ):
                at = (z * X + x) * K
                lines.append(jnp.concatenate([s_ref[h, at : at + K, :] for h in range(2)], 1).astype(BF16))
            term = nt(jnp.concatenate(lines, 0), fl_ref[i])
            total = term if total is None else total + term
        for l in range(u_ref.shape[0]):
            u_ref[l, g] = total[:, l * LANES : (l + 1) * LANES].astype(BF16)


def gram_kernel(K, first, count, s_ref, block_ref, *refs):
    gx_ref = refs[-1]
    leaf_matrix = block_ref[...].astype(BF16)

    def chunk(i, carry):
        gram, mixed = carry
        his = []
        for n in range(NLINES):
            at = pl.multiple_of((first + i * NLINES + n) * K, SUB)
            hi, lo = halves(jnp.concatenate([s_ref[h, pl.ds(at, K), :] for h in range(2)], 1))
            gram = gram + nt(hi, jnp.concatenate([hi, lo], 0))
            his.append(hi)
        leaf = nt(jnp.concatenate(his, 0), leaf_matrix).astype(BF16)
        for n in range(NLINES):
            mixed = mixed + nt(his[n], leaf[n * K : (n + 1) * K])
        return gram, mixed

    init = (jnp.zeros((K, 2 * K), F32), jnp.zeros((K, K), F32))
    gram, mixed = lax.fori_loop(0, count // NLINES, chunk, init, unroll=UNROLL_GRAM)
    low = gram[:, K:]
    gx_ref[...] = jnp.zeros_like(gx_ref)
    gx_ref[:, :K] = gram[:, :K] + low + low.T
    gx_ref[:, LANES // 2 : LANES // 2 + K] = mixed


def couple_kernel(K, parts, u_ref, *refs):
    gx_refs, sib_refs, out_ref = refs[:parts], refs[parts:-1], refs[-1]
    total = jnp.zeros((K, K), F32)
    for l, ref in enumerate(sib_refs):
        for g in range(u_ref.shape[1]):
            for at in range(0, u_ref.shape[2], K):
                total = total + nt(u_ref[l, g, at : at + K, :], ref[g, at : at + K, :])
    out_ref[...] = sum(ref[...] for ref in gx_refs)
    at = LANES // 2
    out_ref[:, at : at + K] = out_ref[:, at : at + K] + total


def eliminated(K, aug):
    tile = (SUB, LANES)
    tiles = [aug[i : i + SUB] for i in range(0, K, SUB)]
    sub = lax.broadcasted_iota(jnp.int32, tile, 0)
    for first in range(K // SUB):
        rest = range(first, K // SUB)
        j = first * SUB
        columns = [[jnp.broadcast_to(tiles[i][:, j + q : j + q + 1], tile) for i in rest] for q in range(SUB)]
        rows = [jnp.broadcast_to(tiles[first][q : q + 1, :], tile) for q in range(SUB)]
        block = [[jnp.broadcast_to(columns[t][0][q : q + 1, :], tile) for t in range(SUB)] for q in range(SUB)]
        for q in range(SUB):
            inverse = 1.0 / block[q][q]
            multiples = [c * inverse for c in columns[q]]
            for t in range(q + 1, SUB):
                factor = block[q][t] * inverse
                for u in range(t, SUB):
                    block[t][u] = block[t][u] - factor * block[q][u]
                rows[t] = rows[t] - factor * rows[q]
                columns[t] = [c - m * block[q][t] for c, m in zip(columns[t], multiples)]
            columns[q] = multiples
        for n, i in enumerate(rest):
            for q in range(SUB):
                m = columns[q][n]
                if n == 0:
                    if q == SUB - 1:
                        continue
                    m = jnp.where(sub > q, m, 0.0)
                tiles[i] = tiles[i] - m * rows[q]
    return jnp.concatenate(tiles, 0)


def finish_kernel(K, NZ, X, cells, gx_ref, s_ref, basis_ref, proj_ref, out, sem):
    lane = lanes_of((K, LANES))
    row = lax.broadcasted_iota(jnp.int32, (K, LANES), 0)
    half = LANES // 2
    gx = gx_ref[...] * (1.0 / cells)
    gram = gx[:, :K]
    mixed = gram + gx[:, half : half + K]
    aug = jnp.where(lane < K, gx, jnp.where(lane - half == row, 1.0, 0.0))
    aug = eliminated(K, aug)
    pivots = jnp.sum(jnp.where(lane == row, aug, 0.0), axis=1, keepdims=True)
    inverse = aug[:, half : half + K] * lax.rsqrt(pivots)
    left = jnp.dot(inverse, mixed, precision=HIGH, preferred_element_type=F32)
    proj_ref[...] = nt(left, inverse, precision=HIGH)
    i_hi, i_lo = halves(inverse)
    lhs = jnp.concatenate([i_hi, i_lo, i_hi], 1)
    copies = []
    for z in range(NZ):

        def line(x, carry, z=z):
            at = pl.multiple_of((z * X + x) * K, SUB)
            s = jnp.concatenate([s_ref[h, pl.ds(at, K), :] for h in range(2)], 1)
            hi, lo = halves(s)
            b = jnp.dot(lhs, jnp.concatenate([hi, hi, lo], 0), preferred_element_type=F32)
            for h in range(2):
                out[h, z, pl.ds(x, K, stride=X), :] = b[:, h * LANES : (h + 1) * LANES]
            return carry

        lax.fori_loop(0, X, line, 0, unroll=True)
        for h in range(2):
            for _ in range(1):
                copies.append(
                    pltpu.make_async_copy(
                        out.at[h, z].reshape(K, X, LANES), basis_ref.at[:, z, :, pl.ds(h * LANES, LANES)], sem.at[z, h]
                    )
                )
                copies[-1].start()
    for c in copies:
        c.wait()


def in_hbm(v):
    return pltpu.with_memory_space_constraint(v, pltpu.HBM)


def exchanged(v, axis, bits):
    return lax.ppermute(v, axis, [(i, i ^ bits) for i in range(lax.axis_size(axis))])


def paired(v, axis, first, ring=True):
    n = lax.axis_size(axis)
    swaps = [(i, i + 1) for i in range(first, n - 1, 2)]
    if first and ring:
        swaps = swaps + [(0, n - 1)]
    return lax.ppermute(v, axis, swaps + [(j, i) for i, j in swaps])


def summed(v):
    n, m = lax.axis_size("gx"), lax.axis_size("gy")
    v = v + exchanged(v, "gy", 1)
    steps = [(0, 2**i) for i in range(1, m.bit_length() - 1)] + [(2**i, 0) for i in range(n.bit_length() - 1)]
    for dx, dy in steps:
        swaps = [(i * m + j, (i ^ dx) * m + (j ^ dy ^ 1)) for i in range(n) for j in range(m)]
        v = v + lax.ppermute(v, ("gx", "gy"), swaps)
    return v


def shards(probes, classes, class_table, weights, prior_block, prior_left, prior_right, block_ranks):
    K, NZ, X, W = probes.shape
    R = prior_left.shape[1]
    levels = lax.axis_size("gy").bit_length() - 1
    cells = float(NZ * X * W * lax.axis_size("gx") * lax.axis_size("gy"))
    rows, ext, wide = NZ * X, X + 4, X + 2
    shape = jax.ShapeDtypeStruct
    cls2, w2 = classes.reshape(rows, W), weights.reshape(rows, W)
    params = functools.partial(pltpu.CompilerParams, vmem_limit_bytes=32 << 20)
    y_rows, x_rows = 2 * K + AUX, 2 * NZ * K
    q_rows = 2 * (K + AUX) + 2 * NZ * SUB
    square = (LANES, LANES)
    per = LANES // R
    groups = X // per

    def cost(flops, nbytes=4 << 20):
        return pl.CostEstimate(flops=flops, bytes_accessed=nbytes, transcendentals=0)

    pt, cg, wg, own, y0, y1 = pl.pallas_call(
        functools.partial(pack_kernel, K, NZ, X),
        out_shape=(
            shape((2, NZ * ext * K, LANES), F32),
            shape((2, *square), F32),
            shape((2, *square), F32),
            shape((2, K, LANES), F32),
            shape((y_rows, LANES), BF16),
            shape((y_rows, LANES), BF16),
        ),
        in_specs=[HBM] * 3,
        out_specs=(VMEM,) * 6,
        scratch_shapes=[
            pltpu.VMEM((K * rows, W), BF16),
            pltpu.VMEM((rows, W), jnp.int32),
            pltpu.VMEM((rows, W), F32),
            pltpu.VMEM((4, K, LANES), F32),
            pltpu.VMEM((2, AUX, LANES), F32),
            pltpu.SemaphoreType.DMA((K // SUB + 2,)),
        ],
        compiler_params=params(),
        name="pack",
    )(in_hbm(probes.reshape(K * rows, W)), in_hbm(cls2), in_hbm(w2))
    y0, y1 = paired(y0, "gy", 0), paired(y1, "gy", 1)
    q0, q1, x0, x1 = pl.pallas_call(
        functools.partial(send_kernel, K, NZ, X),
        out_shape=(shape((q_rows, LANES), BF16),) * 2 + (shape((x_rows, W), BF16),) * 2,
        in_specs=[VMEM] * 5,
        out_specs=(VMEM,) * 4,
        scratch_shapes=[pltpu.VMEM((2 * NZ * SUB, LANES), F32)],
        compiler_params=params(),
        name="send",
    )(pt, cg, wg, y0, y1)
    q0 = paired(q0, "gx", 0)
    q1 = paired(q1, "gx", 1)
    x0 = paired(x0, "gx", 0)
    x1 = paired(x1, "gx", 1, False)
    factors = shape((per, levels * LANES, W), BF16)
    fr, fl = pl.pallas_call(
        functools.partial(prep_kernel, levels, R),
        out_shape=(factors, factors),
        in_specs=[VMEM, pl.BlockSpec(memory_space=pltpu.SMEM), VMEM, VMEM],
        out_specs=(VMEM, VMEM),
        cost_estimate=cost(1 << 20, 2 << 20),
        compiler_params=params(),
        name="prep",
    )(y0, block_ranks, prior_right, prior_left)
    slab = shape((2, rows * K, LANES), F32)
    firsts = shape((2, NZ * wide * K, LANES), F32)
    pair = shape((2, K, LANES), F32)
    coefs = shape((14, 2, *square), F32)
    s, t, cf, hp, ht, acc = pl.pallas_call(
        functools.partial(inner_kernel, K, NZ, X, R),
        out_shape=(slab, firsts, coefs, pair, pair, shape((groups, NZ * K, levels * LANES), F32)),
        in_specs=[HBM] + [VMEM] * 9,
        out_specs=(VMEM,) * 6,
        scratch_shapes=[pltpu.VMEM((4, *square), F32)] * 3
        + [
            pltpu.VMEM((3, 2, y_rows, LANES), F32),
            pltpu.VMEM((2, 2 * NZ * SUB, LANES), F32),
            pltpu.SMEM(class_table.shape, F32),
            pltpu.SemaphoreType.DMA,
        ],
        cost_estimate=cost(1 << 30, 20 << 20),
        compiler_params=params(),
        name="inner",
    )(in_hbm(class_table), pt, y0, y1, q0, q1, own, cg, wg, fr)
    side = shape((levels, groups, NZ * K, LANES), BF16)
    _, _, s, v = pl.pallas_call(
        functools.partial(edge_kernel, K, NZ, X, R),
        out_shape=(shape(pt.shape, F32), firsts, slab, side),
        in_specs=[VMEM] * 10,
        out_specs=(VMEM,) * 4,
        input_output_aliases={0: 0, 1: 1, 2: 2},
        compiler_params=params(),
        name="edge",
    )(pt, t, s, x0, x1, cf, hp, ht, acc, fr)
    share = rows // GRAM_PARTS
    parts = []

    def gram_part(i, *after):
        return pl.pallas_call(
            functools.partial(gram_kernel, K, i * share, share),
            out_shape=shape((K, LANES), F32),
            in_specs=[VMEM] * (2 + len(after)),
            out_specs=VMEM,
            cost_estimate=cost(2 * 300 * K * share * W, 8 << 20),
            compiler_params=params(),
        )(s, prior_block, *after)

    parts.append(gram_part(0))
    sibs = []
    pending = v
    for l in range(levels):
        got = exchanged(pending, "gy", 2**l + (l > 0))
        if l == 0:
            first_got = got
        sibs.append(got[0])
        pending = (pending[1:].astype(F32) + got[1:].astype(F32)).astype(BF16)
    parts += [gram_part(i, first_got) for i in range(1, GRAM_PARTS)]
    u = pl.pallas_call(
        functools.partial(left_kernel, K, NZ, X, R),
        out_shape=side,
        in_specs=[VMEM] * 3,
        out_specs=VMEM,
        cost_estimate=cost(1 << 28, 8 << 20),
        compiler_params=params(),
        name="left",
    )(first_got, s, fl)
    gx = pl.pallas_call(
        functools.partial(couple_kernel, K, GRAM_PARTS),
        out_shape=shape((K, LANES), F32),
        in_specs=[VMEM] * (1 + GRAM_PARTS + levels),
        out_specs=VMEM,
        compiler_params=params(),
        name="couple",
    )(u, *parts, *sibs)
    gx = summed(gx)
    basis, projected = pl.pallas_call(
        functools.partial(finish_kernel, K, NZ, X, cells),
        out_shape=(shape((K, NZ, X, W), F32), shape((K, K), F32)),
        in_specs=[VMEM] * 2,
        out_specs=(HBM, VMEM),
        scratch_shapes=[pltpu.VMEM((2, NZ, K * X, LANES), F32), pltpu.SemaphoreType.DMA((NZ, 2))],
        compiler_params=params(),
        name="finish",
    )(gx, s)
    return basis, projected


def solution(mesh):
    return jax.shard_map(
        shards,
        mesh=mesh,
        in_specs=(
            P(None, None, "gx", "gy"),
            P(None, "gx", "gy"),
            P(),
            P(None, "gx", "gy"),
            P("gy", None),
            P(None, None, "gy"),
            P(None, None, "gy"),
            P(),
        ),
        out_specs=(P(None, None, "gx", "gy"), P()),
        check_vma=False,
    )
```
